32 devices in a mesh: parts: 2 (over y), row: 4 (over z), col: 4 (over x, core).
Axes of the slice: x: 2, y: 2, z: 4, core: 2. Of those that a mesh axis runs over, the one named last changes fastest.
Arguments:
- single: bfloat16 [8, 1024, 768], P(None, ('parts', 'row'), 'col'), parts along dimension 1, may hold values from -6 to 6
- pair_act: bfloat16 [1024, 512, 128], P(('parts', 'row'), 'col'), parts along dimension 0, may hold values from -6 to 6
- token_mask: int32 [1024], P(('parts', 'row')), parts along dimension 0, may hold values 0 or 1
- atom_feats: bfloat16 [8192, 128], P(('parts', 'row', 'col')), parts along dimension 0, may hold values from -6 to 6
- atom_token: int32 [8192], P(('parts', 'row', 'col')), parts along dimension 0, may hold values from 0 to 127, as said below
- atom_count: int32 [32], P(('parts', 'row', 'col')), parts along dimension 0, may hold values from 32 to 256, as said below
- atom_weight: bfloat16 [128, 768], P(None, 'col'), may hold values from -0.5 to 0.5
- bias_weight: bfloat16 [128, 2, 16], replicated, may hold values from -16 to 16
- qkvg_weight: bfloat16 [2, 4, 768, 768], P(None, None, 'col'), may hold values from -0.21875 to 0.21875
- out_weight: bfloat16 [2, 768, 768], P(None, 'col'), may hold values from -0.21875 to 0.21875
Outputs:
- updated: bfloat16 [8, 1024, 768], P(None, ('parts', 'row'), 'col'), parts along dimension 1
The draws below stay inside these ranges and needn't reach their ends.
There are 2 independent parts, one for each index of `parts`. The reference program is written for one: setup_inputs(seed, part) draws one part's arguments, and reference() takes and returns one part's arrays. A program takes and returns all parts, laid end to end along the dimension named above; an argument that names none is the same for every part. Nothing has to cross between parts.
Inputs may be any that keep to these rules, and one draw needn't show every extreme that they name: `atom_token`: slots of a device hold atoms of the 128 tokens of that device's row block, numbered within the block; every token owns at least one live slot. The first atom_count slots of a device are live, the others are padding; in every draw some device has all 256 slots live.
All inputs are finite; a program needn't handle non-finite values. No bound on the sum of `token_mask` on one device may be relied on, other than what follows from the above.
Results may differ from the reference program's by a relative error of at most 0.014.
The reference program's roundings to bfloat16 on the way count: a program that leaves them out, or rounds other values in their place, can miss the bound.
Values may be sent and summed in bfloat16 or wider, within the bound.
A program may use at most 64 MiB of HBM per device.

```python
import math
import jax
import jax.numpy as jnp
from jax import lax

D = 768
HEADS = 16
HEAD_DIM = 48
CZ = 128
CA = 128
LAYERS = 2
SAMPLES = 8
TOK_DEV = 128
ATOM_DEV = 256
TOKENS = 512
GRID = 16
COL_DEVS = 4
TOK_COL = 32
ATOMS = 4096
N_ROW = 4


def draw_pair_act(key, part):
    drawn = jax.random.normal(jax.random.fold_in(key, 1), (TOKENS, TOKENS, CZ), jnp.float32)
    return jnp.clip(drawn, -6.0, 6.0).astype(jnp.bfloat16)


def draw_bias_weight(key, part):
    drawn = jnp.clip(jax.random.normal(jax.random.fold_in(key, 6), (CZ, LAYERS, HEADS), jnp.float32), -6.0, 6.0)
    base = drawn / math.sqrt(CZ)
    return base.astype(jnp.bfloat16)


def draw_atom_count(key, part):
    halvings = jax.random.randint(jax.random.fold_in(key, 11), (GRID,), 0, 4)
    counts = ATOM_DEV // jnp.left_shift(jnp.ones((GRID,), jnp.int32), halvings)
    counts = counts - jax.random.randint(jax.random.fold_in(key, 12), (GRID,), 0, max(ATOM_DEV // 16, 1))
    counts = jnp.maximum(counts, TOK_COL)
    fullest = jax.random.randint(jax.random.fold_in(key, 13), (), 0, GRID)
    return jnp.where(jnp.arange(GRID) == fullest, ATOM_DEV, counts).astype(jnp.int32)


def draw_atom_token(key, part):
    slot_ids = jnp.arange(ATOM_DEV, dtype=jnp.int32)
    column = jnp.arange(GRID, dtype=jnp.int32) % COL_DEVS
    assigned = column[:, None] * TOK_COL + slot_ids[None, :]
    scattered = jax.random.randint(jax.random.fold_in(key, 14), (GRID, ATOM_DEV), 0, TOK_DEV)
    return jnp.where(slot_ids[None, :] < TOK_COL, assigned, scattered).reshape(ATOMS).astype(jnp.int32)


def set_ends(result, key, least, top_value):
    longest = result.shape.index(max(result.shape))
    spots = []
    for shift in (0, 1):
        where = [jax.random.randint(jax.random.fold_in(key, axis), (), 0, length) for axis, length in enumerate(result.shape)]
        where[longest] = (where[longest] + shift) % result.shape[longest]
        spots.append(tuple(where))
    return result.at[spots[0]].set(least).at[spots[1]].set(top_value)


def block_scale(key, shape, cuts, least, high):
    factor_of, own = 1.0, jax.random.fold_in(key, 6)
    for position, shards_of in cuts:
        draws = jnp.exp(jax.random.uniform(jax.random.fold_in(own, position), (shards_of,), jnp.float32, least / len(cuts), high / len(cuts)))
        factor_of = factor_of * jnp.repeat(draws, shape[position] // shards_of).reshape([-1 if axis == position else 1 for axis in range(len(shape))])
    return factor_of


def normal_values(rng, dims, spread, limit, pieces=(), held_as=jnp.bfloat16):
    entries = spread * jax.random.normal(rng, dims, jnp.float32)
    if pieces:
        entries = entries * block_scale(rng, dims, pieces, -0.22, 0.18)
    return jnp.clip(entries, -limit, limit).astype(held_as)


def setup_inputs(seed: int = 0, part: int = 0) -> dict:
    key_of = jax.random.split(jax.random.key(seed), 11)
    own_keys = jax.random.split(jax.random.fold_in(key_of[10], part), 11)
    return {
        "single": normal_values(own_keys[0], (SAMPLES, TOKENS, D), 1.0, 6.0, ((1, 4), (2, 4))),
        "pair_act": draw_pair_act(jax.random.fold_in(jax.random.fold_in(key_of[10], part), 71), part),
        "token_mask": set_ends((jax.random.randint(own_keys[2], (TOKENS,), 0, 16) < 15).astype(jnp.int32), jax.random.fold_in(own_keys[2], 1), 0, 1),
        "atom_feats": normal_values(own_keys[3], (ATOMS, CA), 1.0, 6.0, ((0, 16),)),
        "atom_token": draw_atom_token(jax.random.fold_in(jax.random.fold_in(key_of[10], part), 71), part),
        "atom_count": draw_atom_count(jax.random.fold_in(jax.random.fold_in(key_of[10], part), 71), part),
        "atom_weight": normal_values(key_of[6], (CA, D), CA ** -0.5, 0.5, ((1, 4),)),
        "bias_weight": draw_bias_weight(jax.random.fold_in(key_of[10], 71), part),
        "qkvg_weight": normal_values(key_of[8], (LAYERS, 4, D, D), D ** -0.5, 0.21875, ((2, 4),)),
        "out_weight": normal_values(key_of[9], (LAYERS, D, D), D ** -0.5, 0.21875, ((1, 4),)),
    }


EPS = 1e-05
MASKED = -1000000000.0

def layer_norm(values):
    average = lax.optimization_barrier(jnp.mean(values, axis=-1, keepdims=True))
    centered = values - average
    variance = lax.optimization_barrier(jnp.mean(centered * centered, axis=-1, keepdims=True))
    return centered * lax.rsqrt(variance + EPS)

def reference(single, pair_act, token_mask, atom_feats, atom_token, atom_count, atom_weight, bias_weight, qkvg_weight, out_weight):
    slot_ids = jnp.arange(ATOMS, dtype=jnp.int32)
    device = slot_ids // ATOM_DEV
    live_slots = slot_ids % ATOM_DEV < atom_count[device]
    owners = (device // COL_DEVS * TOK_DEV + atom_token).astype(jnp.int32)
    live_float = live_slots.astype(jnp.float32)
    atom_sums = jax.ops.segment_sum(atom_feats.astype(jnp.float32) * live_float[:, None], owners, num_segments=TOKENS)
    counts = jax.ops.segment_sum(live_float, owners, num_segments=TOKENS)
    pooled = jnp.dot(atom_sums, atom_weight.astype(jnp.float32), precision=lax.Precision.HIGHEST) / counts[:, None]
    stream = (single.astype(jnp.float32) + pooled[None]).astype(jnp.bfloat16)

    def bias_rows(pair_block):
        normed_block = layer_norm(pair_block.astype(jnp.float32)).astype(jnp.bfloat16)
        return jnp.einsum('ijc,clh->lhij', normed_block.astype(jnp.float32), bias_weight.astype(jnp.float32)).astype(jnp.bfloat16)
    blocks = pair_act.reshape(N_ROW, TOK_DEV, TOKENS, CZ)
    biases = lax.map(bias_rows, blocks)
    biases = jnp.moveaxis(biases, 0, 2).reshape(LAYERS, HEADS, TOKENS, TOKENS)
    key_live = token_mask > 0
    score_scale = 1.0 / math.sqrt(HEAD_DIM)

    def head_attention(inputs):
        head_query, head_keys, head_values, head_bias = inputs
        scores = jnp.einsum('sqd,skd->sqk', head_query.astype(jnp.float32), head_keys.astype(jnp.float32)) * score_scale
        scores = scores + head_bias.astype(jnp.float32)[None]
        scores = jnp.where(key_live[None, None, :], scores, MASKED)
        highest = lax.optimization_barrier(jnp.max(scores, axis=-1, keepdims=True))
        exponent = jnp.exp(scores - highest)
        summed = lax.optimization_barrier(jnp.sum(exponent, axis=-1, keepdims=True))
        weights = exponent.astype(jnp.bfloat16)
        return jnp.einsum('sqk,skd->sqd', weights.astype(jnp.float32), head_values.astype(jnp.float32)) / summed
    for layer_idx in range(LAYERS):
        normed = layer_norm(stream.astype(jnp.float32)).astype(jnp.bfloat16)
        projected = jnp.einsum('std,fed->fste', normed.astype(jnp.float32), qkvg_weight[layer_idx].astype(jnp.float32))
        queries = projected[0].astype(jnp.bfloat16).reshape(SAMPLES, TOKENS, HEADS, HEAD_DIM).transpose(2, 0, 1, 3)
        key_rows = projected[1].astype(jnp.bfloat16).reshape(SAMPLES, TOKENS, HEADS, HEAD_DIM).transpose(2, 0, 1, 3)
        value_rows = projected[2].astype(jnp.bfloat16).reshape(SAMPLES, TOKENS, HEADS, HEAD_DIM).transpose(2, 0, 1, 3)
        gating = jax.nn.sigmoid(projected[3])
        attended = lax.map(head_attention, (queries, key_rows, value_rows, biases[layer_idx]))
        attended = attended.transpose(1, 2, 0, 3).reshape(SAMPLES, TOKENS, D)
        gated = (gating * attended).astype(jnp.bfloat16)
        update = jnp.einsum('std,ed->ste', gated.astype(jnp.float32), out_weight[layer_idx].astype(jnp.float32))
        stream = (stream.astype(jnp.float32) + update).astype(jnp.bfloat16)
    return stream
```

```python
import math

import jax
import jax.numpy as jnp
from jax import lax
from jax.experimental import pallas as pl
from jax.experimental.pallas import tpu as pltpu
from jax.sharding import PartitionSpec as P

HEAD_DIM = 48
LAYERS = 2


EPS = 1e-05
MASKED = -1000000000.0
START_LOW = -1e30


def layer_norm(values):
    average = jnp.mean(values, axis=-1, keepdims=True)
    centered = values - average
    variance = jnp.mean(centered * centered, axis=-1, keepdims=True)
    return centered * lax.rsqrt(variance + EPS)


def per_device(
    single,
    pair_act,
    token_mask,
    atom_feats,
    atom_token,
    atom_count,
    atom_weight,
    bias_weight,
    qkvg_weight,
    out_weight,
):
    tok_rows = single.shape[1]
    sample_count = single.shape[0]
    slot_ids = jnp.arange(atom_feats.shape[0], dtype=jnp.int32)
    live_slots = slot_ids < atom_count[0]
    token_ids = jnp.arange(tok_rows, dtype=jnp.int32)
    owner_match = (token_ids[:, None] == atom_token[None, :]) & live_slots[None, :]
    owners = owner_match.astype(jnp.float32)
    counts = jnp.sum(owners, axis=1)
    atom_sums = jnp.dot(
        owner_match.astype(jnp.bfloat16), atom_feats, preferred_element_type=jnp.float32
    )
    sum_total, count_total = (
        lax.psum(atom_sums.astype(jnp.bfloat16), "col").astype(jnp.float32),
        lax.psum(counts[:, None].astype(jnp.bfloat16), "col").astype(jnp.float32),
    )
    pooled = (
        jnp.dot(sum_total, atom_weight.astype(jnp.float32), precision=lax.Precision.HIGHEST)
        / count_total
    )
    stream = (single.astype(jnp.float32) + pooled[None]).astype(jnp.bfloat16)
    pair_normed = layer_norm(pair_act.astype(jnp.float32)).astype(jnp.bfloat16)
    biases = jnp.einsum(
        "ijc,clh->lhij", pair_normed, bias_weight, preferred_element_type=jnp.float32
    ).astype(jnp.bfloat16)
    live_keys = (token_mask > 0).astype(jnp.bfloat16)[None, :]
    score_scale = 1.0 / math.sqrt(HEAD_DIM)
    for layer_idx in range(LAYERS):
        spread = lax.all_to_all(biases[layer_idx], "col", split_axis=0, concat_axis=2, tiled=True)
        gathered = lax.all_gather(stream, "col", axis=2, tiled=True)
        normed = layer_norm(gathered.astype(jnp.float32)).astype(jnp.bfloat16)
        projected = jnp.einsum(
            "std,fed->fste", normed, qkvg_weight[layer_idx], preferred_element_type=jnp.float32
        )
        head_width = projected.shape[3]
        heads_here = head_width // HEAD_DIM
        queries = (
            projected[0].astype(jnp.bfloat16).reshape(sample_count, tok_rows, heads_here, HEAD_DIM)
        )
        key_rows = projected[1].astype(jnp.bfloat16)
        value_rows = projected[2].astype(jnp.bfloat16)
        gating = jax.nn.sigmoid(projected[3])

        def attend(running, incoming, offset, queries=queries, spread=spread):
            top_old, summed_old, acc_old = running
            keys_in, values_in, live_in = incoming
            key_count = keys_in.shape[1]
            keys_heads = keys_in.reshape(sample_count, key_count, heads_here, HEAD_DIM)
            values_heads = values_in.reshape(sample_count, key_count, heads_here, HEAD_DIM)
            scores = (
                jnp.einsum(
                    "sqhd,skhd->shqk", queries, keys_heads, preferred_element_type=jnp.float32
                )
                * score_scale
            )
            scores = scores + spread.astype(jnp.float32)[None]
            scores = jnp.where(live_in[0][None, None, None, :] > 0, scores, MASKED)
            top_new = jnp.maximum(top_old, jnp.max(scores, axis=-1))
            exponent = jnp.exp(scores - top_new[..., None])
            summed_new = jnp.sum(exponent, axis=-1)
            weights = exponent.astype(jnp.bfloat16)
            acc_new = jnp.einsum(
                "shqk,skhd->shqd", weights, values_heads, preferred_element_type=jnp.float32
            )
            return (top_new, summed_new, acc_new)

        start_state = (
            jnp.full((sample_count, heads_here, tok_rows), START_LOW, jnp.float32),
            jnp.zeros((sample_count, heads_here, tok_rows), jnp.float32),
            jnp.zeros((sample_count, heads_here, tok_rows, HEAD_DIM), jnp.float32),
        )
        top_end, summed_end, acc_end = attend(
            start_state,
            (
                lax.all_gather(key_rows, "row", axis=1, tiled=True),
                lax.all_gather(value_rows, "row", axis=1, tiled=True),
                lax.all_gather(live_keys, "row", axis=1, tiled=True),
            ),
            jnp.int32(0),
        )
        attended = acc_end / summed_end[..., None]
        attended = attended.transpose(0, 2, 1, 3).reshape(sample_count, tok_rows, head_width)
        gated = (gating * attended).astype(jnp.bfloat16)
        out_rows = out_weight[layer_idx]

        def project(summed, incoming, offset, out_rows=out_rows):
            return jnp.einsum("std,ed->ste", incoming, out_rows, preferred_element_type=jnp.float32)

        zero_update = jnp.zeros((sample_count, tok_rows, out_rows.shape[0]), jnp.float32)
        update = project(
            zero_update, lax.all_gather(gated, "col", axis=2, tiled=True), jnp.int32(0)
        )
        stream = (stream.astype(jnp.float32) + update).astype(jnp.bfloat16)
    return stream


MESH = pl.DeviceIdType.MESH
NT = (((1,), (1,)), ((), ()))


def remote(src, dst, send_sem, recv_sem, row, col):
    return pltpu.make_async_remote_copy(
        src_ref=src,
        dst_ref=dst,
        send_sem=send_sem,
        recv_sem=recv_sem,
        device_id={"row": row, "col": col},
        device_id_type=MESH,
    )


def fused(
    rows,
    cols,
    bias,
    single,
    feats,
    slot_token,
    slot_count,
    atom_weight,
    mask,
    qkvg,
    out_w,
    out,
    spread,
    normed,
    out_full,
    stream,
    parts_buf,
    stream_send,
    stream_recv,
    mask_buf,
    queries,
    keys,
    values,
    gates,
    gated_send,
    gated_recv,
    final_send,
    part_sems,
    mask_sems,
    a2a_sems,
    ring_sems,
    out_w_sems,
    in_sems,
    ag_sems,
    gated_sems,
    end_sems,
):
    r = lax.axis_index("row")
    c = lax.axis_index("col")
    own = single.shape[0] // rows
    tokens = single.shape[1]
    width = single.shape[2]
    heads = width // HEAD_DIM
    depth = rows * tokens
    sibling = c + 1 - 2 * lax.rem(c, 2)
    across = lax.rem(c + 2, cols)
    far = lax.rem(sibling + 2, cols)
    on_diag = r == c

    barrier = pltpu.get_barrier_semaphore()
    for dr in range(rows):
        for dc in range(cols):
            if dr or dc:
                pl.semaphore_signal(
                    barrier,
                    inc=1,
                    device_id={"row": lax.rem(r + dr, rows), "col": lax.rem(c + dc, cols)},
                    device_id_type=MESH,
                )
    pl.semaphore_wait(barrier, rows * cols - 1)

    sent = []

    def col_of(d):
        return lax.rem(c + d, cols)

    def bias_exchange(l):
        for d in range(1, cols):
            to = col_of(d)
            desc = remote(
                bias.at[l, to],
                spread.at[l, r, c],
                a2a_sems.at[0, l, d],
                a2a_sems.at[1, l, d],
                r,
                to,
            )
            desc.start()
            sent.append(desc)
        spread[l, r, c] = bias[l, c]

    def bias_exchange_wait(l):
        for d in range(1, cols):
            frm = col_of(cols - d)
            remote(
                bias.at[l, frm],
                spread.at[l, r, frm],
                a2a_sems.at[0, l, d],
                a2a_sems.at[1, l, d],
                r,
                frm,
            ).wait_recv()

    def ring_desc(l, right, step, block):
        side = 0 if right else 1
        to = r + 1 if right else r - 1
        return remote(
            spread.at[l, block],
            spread.at[l, block],
            ring_sems.at[0, l, side, step],
            ring_sems.at[1, l, side, step],
            to,
            c,
        )

    def ring_send(l, step):
        @pl.when((r + 1 < rows) & (r - step >= 0))
        def _():
            ring_desc(l, True, step, r - step).start()

        @pl.when((r - 1 >= 0) & (r + step < rows))
        def _():
            ring_desc(l, False, step, r + step).start()

    def ring_sent(l, step):
        @pl.when((r + 1 < rows) & (r - step >= 0))
        def _():
            ring_desc(l, True, step, r - step).wait_send()

        @pl.when((r - 1 >= 0) & (r + step < rows))
        def _():
            ring_desc(l, False, step, r + step).wait_send()

    def advance(l, step):
        @pl.when(r - 1 - step >= 0)
        def _():
            block = r - 1 - step
            remote(
                spread.at[l, block],
                spread.at[l, block],
                ring_sems.at[0, l, 0, step],
                ring_sems.at[1, l, 0, step],
                r - 1,
                c,
            ).wait_recv()

        @pl.when((r - 1 - step >= 0) & (r + 1 < rows) & (step + 1 < rows - 1))
        def _():
            ring_desc(l, True, step + 1, r - step - 1).start()

        @pl.when(r + 1 + step < rows)
        def _():
            block = r + 1 + step
            remote(
                spread.at[l, block],
                spread.at[l, block],
                ring_sems.at[0, l, 1, step],
                ring_sems.at[1, l, 1, step],
                r + 1,
                c,
            ).wait_recv()

        @pl.when((r + 1 + step < rows) & (r - 1 >= 0) & (step + 1 < rows - 1))
        def _():
            ring_desc(l, False, step + 1, r + step + 1).start()

    for d in range(1, rows):
        to = lax.rem(r + d, rows)
        desc = remote(mask, mask_buf.at[r], mask_sems.at[0, d], mask_sems.at[1, d], to, c)
        desc.start()
        sent.append(desc)
    mask_buf[r] = mask[...]

    slots = feats.shape[0]
    token_ids = lax.broadcasted_iota(jnp.int32, (tokens, slots), 0)
    slot_ids = lax.broadcasted_iota(jnp.int32, (tokens, slots), 1)
    match = (token_ids == slot_token[...]) & (slot_ids < slot_count[...])
    owners = jnp.where(match, 1.0, 0.0).astype(jnp.bfloat16)
    parts_buf[c, 0:tokens] = jnp.dot(
        owners, feats[...], preferred_element_type=jnp.float32
    ).astype(jnp.bfloat16)
    parts_buf[c, tokens : tokens + 16] = lax.dot_general(
        jnp.ones((16, slots), jnp.bfloat16), owners, NT, preferred_element_type=jnp.float32
    ).astype(jnp.bfloat16)
    for d in range(1, cols):
        desc = remote(
            parts_buf.at[c], parts_buf.at[c], part_sems.at[0, d], part_sems.at[1, d], r, col_of(d)
        )
        desc.start()
        sent.append(desc)
    bias_exchange(0)
    for d in range(1, cols):
        frm = col_of(cols - d)
        remote(
            parts_buf.at[frm], parts_buf.at[frm], part_sems.at[0, d], part_sems.at[1, d], r, frm
        ).wait_recv()
    total = jnp.zeros((tokens, width), jnp.float32)
    count_row = jnp.zeros((1, tokens), jnp.float32)
    for k in range(cols):
        total = total + jnp.dot(
            parts_buf[k, 0:tokens], atom_weight[...], preferred_element_type=jnp.float32
        )
        count_row = count_row + parts_buf[k, tokens : tokens + 16].astype(jnp.float32)[0:1]
    square = (
        lax.broadcasted_iota(jnp.int32, (tokens, tokens), 0)
        == lax.broadcasted_iota(jnp.int32, (tokens, tokens), 1)
    )
    count_col = jnp.sum(jnp.where(square, count_row, 0.0), axis=1, keepdims=True)
    pooled = total / count_col
    for s in range(single.shape[0]):
        stream_send[s] = (single[s].astype(jnp.float32) + pooled).astype(jnp.bfloat16)
    for d in range(rows):
        to = lax.rem(r + d, rows)
        piece = stream_send.at[pl.ds(to * own, own)]
        if d == 0:

            @pl.when(on_diag)
            def _():
                stream_recv[c] = stream_send[pl.ds(r * own, own)]

            @pl.when(jnp.logical_not(on_diag))
            def _(piece=piece, to=to):
                remote(piece, stream_recv.at[c], in_sems.at[0, 0], in_sems.at[1, c], to, r).start()

        else:
            desc = remote(piece, stream_recv.at[c], in_sems.at[0, d], in_sems.at[1, c], to, r)
            desc.start()
            sent.append(desc)

    bias_exchange_wait(0)
    ring_send(0, 0)
    bias_exchange(1)

    for kind, to in ((0, sibling), (1, across)):
        desc = remote(
            out_w, out_full.at[c], out_w_sems.at[0, kind], out_w_sems.at[1, kind], r, to
        )
        desc.start()
        sent.append(desc)
    out_full[c] = out_w[...]

    for f in range(cols):

        @pl.when(jnp.logical_not(on_diag & (c == f)))
        def _(f=f):
            remote(
                stream_recv.at[f],
                stream_recv.at[f],
                in_sems.at[0, 0],
                in_sems.at[1, f],
                c,
                f,
            ).wait_recv()

    def send_normed(l, s, here):
        average = jnp.mean(here, axis=-1, keepdims=True)
        centered = here - average
        variance = jnp.mean(centered * centered, axis=-1, keepdims=True)
        normed[l, s, c] = (centered * lax.rsqrt(variance + EPS)).astype(jnp.bfloat16)
        for kind, to in ((0, sibling), (1, across)):
            desc = remote(
                normed.at[l, s, c],
                normed.at[l, s, c],
                ag_sems.at[0, l, s, kind],
                ag_sems.at[1, l, s, kind],
                r,
                to,
            )
            desc.start()
            sent.append(desc)

    def forward_normed(l, s):
        remote(
            normed.at[l, s, across],
            normed.at[l, s, across],
            ag_sems.at[0, l, s, 1],
            ag_sems.at[1, l, s, 1],
            r,
            across,
        ).wait_recv()
        desc = remote(
            normed.at[l, s, across],
            normed.at[l, s, across],
            ag_sems.at[0, l, s, 2],
            ag_sems.at[1, l, s, 2],
            r,
            sibling,
        )
        desc.start()
        sent.append(desc)

    def project(l, s):
        for kind, block in ((0, sibling), (2, far)):
            remote(
                normed.at[l, s, block],
                normed.at[l, s, block],
                ag_sems.at[0, l, s, kind],
                ag_sems.at[1, l, s, kind],
                r,
                sibling,
            ).wait_recv()
        here = normed[l, s].reshape(depth, normed.shape[-1])
        for f, target in enumerate((queries, keys, values)):
            target[s] = lax.dot_general(
                here, qkvg[l, f], NT, preferred_element_type=jnp.float32
            ).astype(jnp.bfloat16)
        gates[s] = jax.nn.sigmoid(
            lax.dot_general(here, qkvg[l, 3], NT, preferred_element_type=jnp.float32)
        )

    score_scale = 1.0 / math.sqrt(HEAD_DIM)

    def attend(l, block):
        live = jnp.concatenate([mask_buf[k][0:1] for k in range(rows)], axis=1) > 0
        lane_head = lax.broadcasted_iota(jnp.int32, (tokens, width), 1)

        def one_sample(s, carry):
            rows_at = pl.ds(pl.multiple_of(block * tokens, tokens), tokens)
            query = queries[s, rows_at, :]
            attended = jnp.zeros((tokens, width), jnp.float32)
            for h in range(heads):
                mine = (lane_head >= h * HEAD_DIM) & (lane_head < (h + 1) * HEAD_DIM)
                masked = jnp.where(mine, query.astype(jnp.float32), 0.0).astype(jnp.bfloat16)
                scores = (
                    lax.dot_general(masked, keys[s], NT, preferred_element_type=jnp.float32)
                    * score_scale
                )
                head_bias = jnp.concatenate([spread[l, block, k, h] for k in range(cols)], axis=1)
                scores = scores + head_bias.astype(jnp.float32)
                scores = jnp.where(live, scores, MASKED)
                highest = jnp.max(scores, axis=-1, keepdims=True)
                exponent = jnp.exp(scores - highest)
                summed = jnp.sum(exponent, axis=-1, keepdims=True)
                mixed = jnp.dot(
                    exponent.astype(jnp.bfloat16), values[s], preferred_element_type=jnp.float32
                )
                attended = jnp.where(mine, mixed * (1.0 / summed), attended)
            gated_send[l, block, s] = (gates[s, rows_at, :] * attended).astype(jnp.bfloat16)
            return carry

        lax.fori_loop(0, own, one_sample, 0)

        gap = lax.rem(block - c + cols, cols)

        @pl.when(block != c)
        def _():
            remote(
                gated_send.at[l, block],
                gated_recv.at[l, c],
                gated_sems.at[0, l, gap],
                gated_sems.at[1, l, gap],
                r,
                block,
            ).start()

        @pl.when(block == c)
        def _():
            gated_recv[l, c] = gated_send[l, block]

    def gated_wait(l):
        for d in range(1, cols):
            frm = col_of(cols - d)
            remote(
                gated_send.at[l, frm],
                gated_recv.at[l, frm],
                gated_sems.at[0, l, d],
                gated_sems.at[1, l, d],
                r,
                frm,
            ).wait_recv()

    for d in range(1, rows):
        frm = lax.rem(r + rows - d, rows)
        remote(
            mask, mask_buf.at[frm], mask_sems.at[0, d], mask_sems.at[1, d], frm, c
        ).wait_recv()

    for s in range(own):
        here = jnp.concatenate([stream_recv[f, s].astype(jnp.float32) for f in range(cols)], axis=1)
        stream[s] = here
        send_normed(0, s, here)

    for l in range(LAYERS):
        if l > 0:
            advance(l, 0)
        for s in range(own):
            forward_normed(l, s)
        for s in range(own):
            project(l, s)
        if l == 0:
            advance(l, 0)
            remote(
                out_w, out_full.at[across], out_w_sems.at[0, 1], out_w_sems.at[1, 1], r, across
            ).wait_recv()
            desc = remote(
                out_full.at[across],
                out_full.at[across],
                out_w_sems.at[0, 2],
                out_w_sems.at[1, 2],
                r,
                sibling,
            )
            desc.start()
            sent.append(desc)

        def ring_round(t, carry, l=l):
            def side(k, inner):
                block = r - t + 2 * t * k

                @pl.when((block >= 0) & (block < rows) & (k <= t))
                def _():
                    attend(l, block)

                return inner

            lax.fori_loop(0, 2, side, 0)

            @pl.when((t >= 1) & (t < rows - 1))
            def _():
                advance(l, t)

            return carry

        lax.fori_loop(0, rows, ring_round, 0)
        if l + 1 < LAYERS:
            bias_exchange_wait(l + 1)
            ring_send(l + 1, 0)
        if l == 0:
            for kind, block in ((0, sibling), (2, far)):
                remote(
                    out_w,
                    out_full.at[block],
                    out_w_sems.at[0, kind],
                    out_w_sems.at[1, kind],
                    r,
                    sibling,
                ).wait_recv()
        gated_wait(l)
        for s in range(own):
            joined = jnp.concatenate(
                [gated_recv[l, k, s].astype(jnp.float32) for k in range(cols)], axis=1
            ).astype(jnp.bfloat16)
            weight = jnp.concatenate([out_full[k, l] for k in range(cols)], axis=0)
            here = stream[s] + lax.dot_general(
                joined, weight, NT, preferred_element_type=jnp.float32
            )
            rounded = here.astype(jnp.bfloat16)
            here = rounded.astype(jnp.float32)
            if l + 1 < LAYERS:
                stream[s] = here
                send_normed(l + 1, s, here)
            else:
                for f in range(cols):
                    final_send[f, s] = here[:, f * width : (f + 1) * width].astype(jnp.bfloat16)

    place = pl.ds(r * own, own)

    def end_desc(f):
        return remote(final_send.at[f], out.at[place], end_sems.at[0, f], end_sems.at[1, r], c, f)

    for f in range(cols):
        stays = on_diag & (c == f)

        @pl.when(stays)
        def _(f=f):
            out[place] = final_send[f]

        @pl.when(jnp.logical_not(stays))
        def _(f=f):
            end_desc(f).start()

    for k in range(rows):

        @pl.when(jnp.logical_not(on_diag & (r == k)))
        def _(k=k):
            remote(
                final_send.at[0],
                out.at[pl.ds(k * own, own)],
                end_sems.at[0, 0],
                end_sems.at[1, k],
                k,
                r,
            ).wait_recv()

    for f in range(cols):

        @pl.when(jnp.logical_not(on_diag & (c == f)))
        def _(f=f):
            end_desc(f).wait_send()

    for desc in sent:
        desc.wait_send()

    @pl.when(jnp.logical_not(on_diag))
    def _():
        remote(
            stream_send.at[pl.ds(r * own, own)],
            stream_recv.at[c],
            in_sems.at[0, 0],
            in_sems.at[1, c],
            r,
            r,
        ).wait_send()

    for l in range(LAYERS):
        for step in range(rows - 1):
            ring_sent(l, step)
        for d in range(1, cols):
            to = col_of(d)
            remote(
                gated_send.at[l, to],
                gated_recv.at[l, c],
                gated_sems.at[0, l, d],
                gated_sems.at[1, l, d],
                r,
                to,
            ).wait_send()


def per_device_fused(
    rows,
    cols,
    single,
    pair_act,
    token_mask,
    atom_feats,
    atom_token,
    atom_count,
    atom_weight,
    bias_weight,
    qkvg_weight,
    out_weight,
):
    samples, tokens, width = single.shape
    own = samples // rows
    depth = rows * tokens
    heads = width // HEAD_DIM
    full = width * cols
    chans = atom_feats.shape[1]
    slots = atom_feats.shape[0]
    pair_normed = layer_norm(pair_act.astype(jnp.float32)).astype(jnp.bfloat16)
    biases = (
        jnp.einsum("ijc,clh->lhij", pair_normed, bias_weight, preferred_element_type=jnp.float32)
        .astype(jnp.bfloat16)
        .reshape(LAYERS, cols, heads, tokens, tokens)
    )
    mask = jnp.broadcast_to((token_mask > 0).astype(jnp.float32)[None, :], (8, tokens))
    bf16, f32 = jnp.bfloat16, jnp.float32
    dma = pltpu.SemaphoreType.DMA
    return pl.pallas_call(
        lambda *refs: fused(rows, cols, *refs),
        out_shape=jax.ShapeDtypeStruct(single.shape, bf16),
        in_specs=[pl.BlockSpec(memory_space=pltpu.VMEM)] * 9,
        out_specs=pl.BlockSpec(memory_space=pltpu.VMEM),
        scratch_shapes=[
            pltpu.VMEM((LAYERS, rows, cols, heads, tokens, tokens), bf16),
            pltpu.VMEM((LAYERS, own, cols, tokens, full), bf16),
            pltpu.VMEM((cols, LAYERS, width, full), bf16),
            pltpu.VMEM((own, tokens, full), f32),
            pltpu.VMEM((cols, tokens + 16, chans), bf16),
            pltpu.VMEM((samples, tokens, width), bf16),
            pltpu.VMEM((cols, own, tokens, width), bf16),
            pltpu.VMEM((rows, 8, tokens), f32),
            pltpu.VMEM((own, depth, width), bf16),
            pltpu.VMEM((own, depth, width), bf16),
            pltpu.VMEM((own, depth, width), bf16),
            pltpu.VMEM((own, depth, width), f32),
            pltpu.VMEM((LAYERS, rows, own, tokens, width), bf16),
            pltpu.VMEM((LAYERS, cols, own, tokens, width), bf16),
            pltpu.VMEM((cols, own, tokens, width), bf16),
            dma((2, cols)),
            dma((2, rows)),
            dma((2, LAYERS, cols)),
            dma((2, LAYERS, 2, rows)),
            dma((2, 3)),
            dma((2, max(rows, cols))),
            dma((2, LAYERS, own, 3)),
            dma((2, LAYERS, cols)),
            dma((2, max(rows, cols))),
        ],
        compiler_params=pltpu.CompilerParams(
            collective_id=0, has_side_effects=True, vmem_limit_bytes=56 * 1024 * 1024
        ),
        name="fused_blocks",
    )(
        biases,
        single,
        atom_feats,
        atom_token.reshape(1, slots),
        atom_count.reshape(1, 1),
        atom_weight,
        mask,
        qkvg_weight,
        out_weight,
    )


def solution(mesh):
    rows, cols = mesh.shape["row"], mesh.shape["col"]
    placed = (
        P(None, ("parts", "row"), "col"),
        P(("parts", "row"), "col", None),
        P(("parts", "row")),
        P(("parts", "row", "col"), None),
        P(("parts", "row", "col")),
        P(("parts", "row", "col")),
        P(None, "col"),
        P(),
        P(None, None, "col", None),
        P(None, "col", None),
    )

    def body(single, *rest):
        pairs = rest[0].shape
        square = rows == cols == 4 and single.shape[0] % rows == 0 and pairs[0] == pairs[1]
        if square and single.shape[2] % HEAD_DIM == 0:
            return per_device_fused(rows, cols, single, *rest)
        return per_device(single, *rest)

    return jax.shard_map(
        body,
        mesh=mesh,
        in_specs=placed,
        out_specs=P(None, ("parts", "row"), "col"),
        check_vma=False,
    )
```

```python
import math

import jax
import jax.numpy as jnp
from jax import lax
from jax.experimental import pallas as pl
from jax.experimental.pallas import tpu as pltpu
from jax.sharding import PartitionSpec as P

HEAD_DIM = 48
LAYERS = 2


EPS = 1e-05
MASKED = -1000000000.0
START_LOW = -1e30


def layer_norm(values):
    average = jnp.mean(values, axis=-1, keepdims=True)
    centered = values - average
    variance = jnp.mean(centered * centered, axis=-1, keepdims=True)
    return centered * lax.rsqrt(variance + EPS)


def per_device(
    single,
    pair_act,
    token_mask,
    atom_feats,
    atom_token,
    atom_count,
    atom_weight,
    bias_weight,
    qkvg_weight,
    out_weight,
):
    tok_rows = single.shape[1]
    sample_count = single.shape[0]
    slot_ids = jnp.arange(atom_feats.shape[0], dtype=jnp.int32)
    live_slots = slot_ids < atom_count[0]
    token_ids = jnp.arange(tok_rows, dtype=jnp.int32)
    owner_match = (token_ids[:, None] == atom_token[None, :]) & live_slots[None, :]
    owners = owner_match.astype(jnp.float32)
    counts = jnp.sum(owners, axis=1)
    atom_sums = jnp.dot(
        owner_match.astype(jnp.bfloat16), atom_feats, preferred_element_type=jnp.float32
    )
    sum_total, count_total = (
        lax.psum(atom_sums.astype(jnp.bfloat16), "col").astype(jnp.float32),
        lax.psum(counts[:, None].astype(jnp.bfloat16), "col").astype(jnp.float32),
    )
    pooled = (
        jnp.dot(sum_total, atom_weight.astype(jnp.float32), precision=lax.Precision.HIGHEST)
        / count_total
    )
    stream = (single.astype(jnp.float32) + pooled[None]).astype(jnp.bfloat16)
    pair_normed = layer_norm(pair_act.astype(jnp.float32)).astype(jnp.bfloat16)
    biases = jnp.einsum(
        "ijc,clh->lhij", pair_normed, bias_weight, preferred_element_type=jnp.float32
    ).astype(jnp.bfloat16)
    live_keys = (token_mask > 0).astype(jnp.bfloat16)[None, :]
    score_scale = 1.0 / math.sqrt(HEAD_DIM)
    for layer_idx in range(LAYERS):
        spread = lax.all_to_all(biases[layer_idx], "col", split_axis=0, concat_axis=2, tiled=True)
        gathered = lax.all_gather(stream, "col", axis=2, tiled=True)
        normed = layer_norm(gathered.astype(jnp.float32)).astype(jnp.bfloat16)
        projected = jnp.einsum(
            "std,fed->fste", normed, qkvg_weight[layer_idx], preferred_element_type=jnp.float32
        )
        head_width = projected.shape[3]
        heads_here = head_width // HEAD_DIM
        queries = (
            projected[0].astype(jnp.bfloat16).reshape(sample_count, tok_rows, heads_here, HEAD_DIM)
        )
        key_rows = projected[1].astype(jnp.bfloat16)
        value_rows = projected[2].astype(jnp.bfloat16)
        gating = jax.nn.sigmoid(projected[3])

        def attend(running, incoming, offset, queries=queries, spread=spread):
            top_old, summed_old, acc_old = running
            keys_in, values_in, live_in = incoming
            key_count = keys_in.shape[1]
            keys_heads = keys_in.reshape(sample_count, key_count, heads_here, HEAD_DIM)
            values_heads = values_in.reshape(sample_count, key_count, heads_here, HEAD_DIM)
            scores = (
                jnp.einsum(
                    "sqhd,skhd->shqk", queries, keys_heads, preferred_element_type=jnp.float32
                )
                * score_scale
            )
            scores = scores + spread.astype(jnp.float32)[None]
            scores = jnp.where(live_in[0][None, None, None, :] > 0, scores, MASKED)
            top_new = jnp.maximum(top_old, jnp.max(scores, axis=-1))
            exponent = jnp.exp(scores - top_new[..., None])
            summed_new = jnp.sum(exponent, axis=-1)
            weights = exponent.astype(jnp.bfloat16)
            acc_new = jnp.einsum(
                "shqk,skhd->shqd", weights, values_heads, preferred_element_type=jnp.float32
            )
            return (top_new, summed_new, acc_new)

        start_state = (
            jnp.full((sample_count, heads_here, tok_rows), START_LOW, jnp.float32),
            jnp.zeros((sample_count, heads_here, tok_rows), jnp.float32),
            jnp.zeros((sample_count, heads_here, tok_rows, HEAD_DIM), jnp.float32),
        )
        top_end, summed_end, acc_end = attend(
            start_state,
            (
                lax.all_gather(key_rows, "row", axis=1, tiled=True),
                lax.all_gather(value_rows, "row", axis=1, tiled=True),
                lax.all_gather(live_keys, "row", axis=1, tiled=True),
            ),
            jnp.int32(0),
        )
        attended = acc_end / summed_end[..., None]
        attended = attended.transpose(0, 2, 1, 3).reshape(sample_count, tok_rows, head_width)
        gated = (gating * attended).astype(jnp.bfloat16)
        out_rows = out_weight[layer_idx]

        def project(summed, incoming, offset, out_rows=out_rows):
            return jnp.einsum("std,ed->ste", incoming, out_rows, preferred_element_type=jnp.float32)

        zero_update = jnp.zeros((sample_count, tok_rows, out_rows.shape[0]), jnp.float32)
        update = project(
            zero_update, lax.all_gather(gated, "col", axis=2, tiled=True), jnp.int32(0)
        )
        stream = (stream.astype(jnp.float32) + update).astype(jnp.bfloat16)
    return stream


MESH = pl.DeviceIdType.MESH
NT = (((1,), (1,)), ((), ()))


def remote(src, dst, send_sem, recv_sem, row, col):
    return pltpu.make_async_remote_copy(
        src_ref=src,
        dst_ref=dst,
        send_sem=send_sem,
        recv_sem=recv_sem,
        device_id={"row": row, "col": col},
        device_id_type=MESH,
    )


def fused(
    rows,
    cols,
    bias,
    single,
    feats,
    slot_token,
    slot_count,
    atom_weight,
    mask,
    qkvg,
    out_w,
    out,
    spread,
    normed,
    out_full,
    stream,
    parts_buf,
    stream_send,
    stream_recv,
    mask_buf,
    queries,
    keys,
    values,
    gates,
    gated_send,
    gated_recv,
    final_send,
    part_sems,
    mask_sems,
    a2a_sems,
    ring_sems,
    out_w_sems,
    in_sems,
    ag_sems,
    gated_sems,
    end_sems,
):
    r = lax.axis_index("row")
    c = lax.axis_index("col")
    own = single.shape[0] // rows
    tokens = single.shape[1]
    width = single.shape[2]
    heads = width // HEAD_DIM
    depth = rows * tokens
    sibling = c + 1 - 2 * lax.rem(c, 2)
    across = lax.rem(c + 2, cols)
    far = lax.rem(sibling + 2, cols)
    on_diag = r == c

    barrier = pltpu.get_barrier_semaphore()
    for dr in range(rows):
        for dc in range(cols):
            if dr or dc:
                pl.semaphore_signal(
                    barrier,
                    inc=1,
                    device_id={"row": lax.rem(r + dr, rows), "col": lax.rem(c + dc, cols)},
                    device_id_type=MESH,
                )
    pl.semaphore_wait(barrier, rows * cols - 1)

    sent = []

    def col_of(d):
        return lax.rem(c + d, cols)

    def bias_exchange(l):
        for d in range(1, cols):
            to = col_of(d)
            desc = remote(
                bias.at[l, to],
                spread.at[l, r, c],
                a2a_sems.at[0, l, d],
                a2a_sems.at[1, l, d],
                r,
                to,
            )
            desc.start()
            sent.append(desc)
        spread[l, r, c] = bias[l, c]

    def bias_exchange_wait(l):
        for d in range(1, cols):
            frm = col_of(cols - d)
            remote(
                bias.at[l, frm],
                spread.at[l, r, frm],
                a2a_sems.at[0, l, d],
                a2a_sems.at[1, l, d],
                r,
                frm,
            ).wait_recv()

    def ring_desc(l, right, step, block):
        side = 0 if right else 1
        to = r + 1 if right else r - 1
        return remote(
            spread.at[l, block],
            spread.at[l, block],
            ring_sems.at[0, l, side, step],
            ring_sems.at[1, l, side, step],
            to,
            c,
        )

    def ring_send(l, step):
        @pl.when((r + 1 < rows) & (r - step >= 0))
        def _():
            ring_desc(l, True, step, r - step).start()

        @pl.when((r - 1 >= 0) & (r + step < rows))
        def _():
            ring_desc(l, False, step, r + step).start()

    def ring_sent(l, step):
        @pl.when((r + 1 < rows) & (r - step >= 0))
        def _():
            ring_desc(l, True, step, r - step).wait_send()

        @pl.when((r - 1 >= 0) & (r + step < rows))
        def _():
            ring_desc(l, False, step, r + step).wait_send()

    def advance(l, step):
        @pl.when(r - 1 - step >= 0)
        def _():
            block = r - 1 - step
            remote(
                spread.at[l, block],
                spread.at[l, block],
                ring_sems.at[0, l, 0, step],
                ring_sems.at[1, l, 0, step],
                r - 1,
                c,
            ).wait_recv()

        @pl.when((r - 1 - step >= 0) & (r + 1 < rows) & (step + 1 < rows - 1))
        def _():
            ring_desc(l, True, step + 1, r - step - 1).start()

        @pl.when(r + 1 + step < rows)
        def _():
            block = r + 1 + step
            remote(
                spread.at[l, block],
                spread.at[l, block],
                ring_sems.at[0, l, 1, step],
                ring_sems.at[1, l, 1, step],
                r + 1,
                c,
            ).wait_recv()

        @pl.when((r + 1 + step < rows) & (r - 1 >= 0) & (step + 1 < rows - 1))
        def _():
            ring_desc(l, False, step + 1, r + step + 1).start()

    for d in range(1, rows):
        to = lax.rem(r + d, rows)
        desc = remote(mask, mask_buf.at[r], mask_sems.at[0, d], mask_sems.at[1, d], to, c)
        desc.start()
        sent.append(desc)
    mask_buf[r] = mask[...]

    slots = feats.shape[0]
    token_ids = lax.broadcasted_iota(jnp.int32, (tokens, slots), 0)
    slot_ids = lax.broadcasted_iota(jnp.int32, (tokens, slots), 1)
    match = (token_ids == slot_token[...]) & (slot_ids < slot_count[...])
    owners = jnp.where(match, 1.0, 0.0).astype(jnp.bfloat16)
    parts_buf[c, 0:tokens] = jnp.dot(
        owners, feats[...], preferred_element_type=jnp.float32
    ).astype(jnp.bfloat16)
    parts_buf[c, tokens : tokens + 16] = lax.dot_general(
        jnp.ones((16, slots), jnp.bfloat16), owners, NT, preferred_element_type=jnp.float32
    ).astype(jnp.bfloat16)
    for d in range(1, cols):
        desc = remote(
            parts_buf.at[c], parts_buf.at[c], part_sems.at[0, d], part_sems.at[1, d], r, col_of(d)
        )
        desc.start()
        sent.append(desc)
    bias_exchange(0)
    for d in range(1, cols):
        frm = col_of(cols - d)
        remote(
            parts_buf.at[frm], parts_buf.at[frm], part_sems.at[0, d], part_sems.at[1, d], r, frm
        ).wait_recv()
    total = jnp.zeros((tokens, width), jnp.float32)
    count_row = jnp.zeros((1, tokens), jnp.float32)
    for k in range(cols):
        total = total + jnp.dot(
            parts_buf[k, 0:tokens], atom_weight[...], preferred_element_type=jnp.float32
        )
        count_row = count_row + parts_buf[k, tokens : tokens + 16].astype(jnp.float32)[0:1]
    square = (
        lax.broadcasted_iota(jnp.int32, (tokens, tokens), 0)
        == lax.broadcasted_iota(jnp.int32, (tokens, tokens), 1)
    )
    count_col = jnp.sum(jnp.where(square, count_row, 0.0), axis=1, keepdims=True)
    pooled = total / count_col
    for s in range(single.shape[0]):
        stream_send[s] = (single[s].astype(jnp.float32) + pooled).astype(jnp.bfloat16)
    for d in range(rows):
        to = lax.rem(r + d, rows)
        piece = stream_send.at[pl.ds(to * own, own)]
        if d == 0:

            @pl.when(on_diag)
            def _():
                stream_recv[c] = stream_send[pl.ds(r * own, own)]

            @pl.when(jnp.logical_not(on_diag))
            def _(piece=piece, to=to):
                remote(piece, stream_recv.at[c], in_sems.at[0, 0], in_sems.at[1, c], to, r).start()

        else:
            desc = remote(piece, stream_recv.at[c], in_sems.at[0, d], in_sems.at[1, c], to, r)
            desc.start()
            sent.append(desc)

    bias_exchange_wait(0)
    ring_send(0, 0)

    def out_w_send(l):
        for kind, to in ((0, sibling), (1, across)):
            desc = remote(
                out_w.at[l],
                out_full.at[c, l],
                out_w_sems.at[0, l, kind],
                out_w_sems.at[1, l, kind],
                r,
                to,
            )
            desc.start()
            sent.append(desc)
        out_full[c, l] = out_w[l]

    def out_w_arrived(l, kind, block):
        remote(
            out_w.at[l],
            out_full.at[block, l],
            out_w_sems.at[0, l, kind],
            out_w_sems.at[1, l, kind],
            r,
            sibling,
        ).wait_recv()

    for f in range(cols):

        @pl.when(jnp.logical_not(on_diag & (c == f)))
        def _(f=f):
            remote(
                stream_recv.at[f],
                stream_recv.at[f],
                in_sems.at[0, 0],
                in_sems.at[1, f],
                c,
                f,
            ).wait_recv()

    def send_normed(l, s, here):
        average = jnp.mean(here, axis=-1, keepdims=True)
        centered = here - average
        variance = jnp.mean(centered * centered, axis=-1, keepdims=True)
        normed[l, s, c] = (centered * lax.rsqrt(variance + EPS)).astype(jnp.bfloat16)
        for kind, to in ((0, sibling), (1, across)):
            desc = remote(
                normed.at[l, s, c],
                normed.at[l, s, c],
                ag_sems.at[0, l, s, kind],
                ag_sems.at[1, l, s, kind],
                r,
                to,
            )
            desc.start()
            sent.append(desc)

    def forward_normed(l, s):
        remote(
            normed.at[l, s, across],
            normed.at[l, s, across],
            ag_sems.at[0, l, s, 1],
            ag_sems.at[1, l, s, 1],
            r,
            across,
        ).wait_recv()
        desc = remote(
            normed.at[l, s, across],
            normed.at[l, s, across],
            ag_sems.at[0, l, s, 2],
            ag_sems.at[1, l, s, 2],
            r,
            sibling,
        )
        desc.start()
        sent.append(desc)

    def project(l, s):
        for kind, block in ((0, sibling), (2, far)):
            remote(
                normed.at[l, s, block],
                normed.at[l, s, block],
                ag_sems.at[0, l, s, kind],
                ag_sems.at[1, l, s, kind],
                r,
                sibling,
            ).wait_recv()
        here = normed[l, s].reshape(depth, normed.shape[-1])
        for f, target in enumerate((queries, keys, values)):
            target[s] = lax.dot_general(
                here, qkvg[l, f], NT, preferred_element_type=jnp.float32
            ).astype(jnp.bfloat16)
        gates[s] = jax.nn.sigmoid(
            lax.dot_general(here, qkvg[l, 3], NT, preferred_element_type=jnp.float32)
        )

    score_scale = 1.0 / math.sqrt(HEAD_DIM)

    def attend(l, block):
        live = jnp.concatenate([mask_buf[k][0:1] for k in range(rows)], axis=1) > 0
        lane_head = lax.broadcasted_iota(jnp.int32, (tokens, width), 1)

        def one_sample(s, carry):
            rows_at = pl.ds(pl.multiple_of(block * tokens, tokens), tokens)
            query = queries[s, rows_at, :]
            attended = jnp.zeros((tokens, width), jnp.float32)
            for h in range(heads):
                mine = (lane_head >= h * HEAD_DIM) & (lane_head < (h + 1) * HEAD_DIM)
                masked = jnp.where(mine, query.astype(jnp.float32), 0.0).astype(jnp.bfloat16)
                scores = (
                    lax.dot_general(masked, keys[s], NT, preferred_element_type=jnp.float32)
                    * score_scale
                )
                head_bias = jnp.concatenate([spread[l, block, k, h] for k in range(cols)], axis=1)
                scores = scores + head_bias.astype(jnp.float32)
                scores = jnp.where(live, scores, MASKED)
                highest = jnp.max(scores, axis=-1, keepdims=True)
                exponent = jnp.exp(scores - highest)
                summed = jnp.sum(exponent, axis=-1, keepdims=True)
                mixed = jnp.dot(
                    exponent.astype(jnp.bfloat16), values[s], preferred_element_type=jnp.float32
                )
                attended = jnp.where(mine, mixed * (1.0 / summed), attended)
            gated_send[l, block, s] = (gates[s, rows_at, :] * attended).astype(jnp.bfloat16)
            return carry

        lax.fori_loop(0, own, one_sample, 0)

        gap = lax.rem(block - c + cols, cols)

        @pl.when(block != c)
        def _():
            remote(
                gated_send.at[l, block],
                gated_recv.at[l, c],
                gated_sems.at[0, l, gap],
                gated_sems.at[1, l, gap],
                r,
                block,
            ).start()

        @pl.when(block == c)
        def _():
            gated_recv[l, c] = gated_send[l, block]

    def gated_wait(l):
        for d in range(1, cols):
            frm = col_of(cols - d)
            remote(
                gated_send.at[l, frm],
                gated_recv.at[l, frm],
                gated_sems.at[0, l, d],
                gated_sems.at[1, l, d],
                r,
                frm,
            ).wait_recv()

    for d in range(1, rows):
        frm = lax.rem(r + rows - d, rows)
        remote(
            mask, mask_buf.at[frm], mask_sems.at[0, d], mask_sems.at[1, d], frm, c
        ).wait_recv()

    for s in range(own):
        here = jnp.concatenate([stream_recv[f, s].astype(jnp.float32) for f in range(cols)], axis=1)
        stream[s] = here
        send_normed(0, s, here)

    for l in range(LAYERS):
        for s in range(own):
            forward_normed(l, s)
            if s == 0:
                advance(l, 0)
        if l + 1 < LAYERS:
            bias_exchange(l + 1)
        out_w_send(l)
        for s in range(own):
            project(l, s)

        def ring_round(t, carry, l=l):
            def side(k, inner):
                block = r - t + 2 * t * k

                @pl.when((block >= 0) & (block < rows) & (k <= t))
                def _():
                    attend(l, block)

                return inner

            lax.fori_loop(0, 2, side, 0)

            @pl.when((t >= 1) & (t < rows - 1))
            def _():
                advance(l, t)

            @pl.when(t == rows - 2)
            def _():
                if l + 1 < LAYERS:
                    bias_exchange_wait(l + 1)
                    ring_send(l + 1, 0)

            @pl.when(t == 1)
            def _():
                out_w_arrived(l, 1, across)
                remote(
                    out_full.at[across, l],
                    out_full.at[across, l],
                    out_w_sems.at[0, l, 2],
                    out_w_sems.at[1, l, 2],
                    r,
                    sibling,
                ).start()

            return carry

        lax.fori_loop(0, rows, ring_round, 0)
        out_w_arrived(l, 0, sibling)
        out_w_arrived(l, 2, far)
        gated_wait(l)
        for s in range(own):
            joined = jnp.concatenate(
                [gated_recv[l, k, s].astype(jnp.float32) for k in range(cols)], axis=1
            ).astype(jnp.bfloat16)
            weight = jnp.concatenate([out_full[k, l] for k in range(cols)], axis=0)
            here = stream[s] + lax.dot_general(
                joined, weight, NT, preferred_element_type=jnp.float32
            )
            rounded = here.astype(jnp.bfloat16)
            here = rounded.astype(jnp.float32)
            if l + 1 < LAYERS:
                stream[s] = here
                send_normed(l + 1, s, here)
            else:
                for f in range(cols):
                    final_send[f, s] = here[:, f * width : (f + 1) * width].astype(jnp.bfloat16)

    place = pl.ds(r * own, own)

    def end_desc(f):
        return remote(final_send.at[f], out.at[place], end_sems.at[0, f], end_sems.at[1, r], c, f)

    for f in range(cols):
        stays = on_diag & (c == f)

        @pl.when(stays)
        def _(f=f):
            out[place] = final_send[f]

        @pl.when(jnp.logical_not(stays))
        def _(f=f):
            end_desc(f).start()

    for k in range(rows):

        @pl.when(jnp.logical_not(on_diag & (r == k)))
        def _(k=k):
            remote(
                final_send.at[0],
                out.at[pl.ds(k * own, own)],
                end_sems.at[0, 0],
                end_sems.at[1, k],
                k,
                r,
            ).wait_recv()

    for f in range(cols):

        @pl.when(jnp.logical_not(on_diag & (c == f)))
        def _(f=f):
            end_desc(f).wait_send()

    for desc in sent:
        desc.wait_send()

    @pl.when(jnp.logical_not(on_diag))
    def _():
        remote(
            stream_send.at[pl.ds(r * own, own)],
            stream_recv.at[c],
            in_sems.at[0, 0],
            in_sems.at[1, c],
            r,
            r,
        ).wait_send()

    for l in range(LAYERS):
        remote(
            out_full.at[across, l],
            out_full.at[across, l],
            out_w_sems.at[0, l, 2],
            out_w_sems.at[1, l, 2],
            r,
            sibling,
        ).wait_send()
        for step in range(rows - 1):
            ring_sent(l, step)
        for d in range(1, cols):
            to = col_of(d)
            remote(
                gated_send.at[l, to],
                gated_recv.at[l, c],
                gated_sems.at[0, l, d],
                gated_sems.at[1, l, d],
                r,
                to,
            ).wait_send()


def per_device_fused(
    rows,
    cols,
    single,
    pair_act,
    token_mask,
    atom_feats,
    atom_token,
    atom_count,
    atom_weight,
    bias_weight,
    qkvg_weight,
    out_weight,
):
    samples, tokens, width = single.shape
    own = samples // rows
    depth = rows * tokens
    heads = width // HEAD_DIM
    full = width * cols
    chans = atom_feats.shape[1]
    slots = atom_feats.shape[0]
    pair_normed = layer_norm(pair_act.astype(jnp.float32)).astype(jnp.bfloat16)
    biases = (
        jnp.einsum("ijc,clh->lhij", pair_normed, bias_weight, preferred_element_type=jnp.float32)
        .astype(jnp.bfloat16)
        .reshape(LAYERS, cols, heads, tokens, tokens)
    )
    mask = jnp.broadcast_to((token_mask > 0).astype(jnp.float32)[None, :], (8, tokens))
    bf16, f32 = jnp.bfloat16, jnp.float32
    dma = pltpu.SemaphoreType.DMA
    return pl.pallas_call(
        lambda *refs: fused(rows, cols, *refs),
        out_shape=jax.ShapeDtypeStruct(single.shape, bf16),
        in_specs=[pl.BlockSpec(memory_space=pltpu.VMEM)] * 9,
        out_specs=pl.BlockSpec(memory_space=pltpu.VMEM),
        scratch_shapes=[
            pltpu.VMEM((LAYERS, rows, cols, heads, tokens, tokens), bf16),
            pltpu.VMEM((LAYERS, own, cols, tokens, full), bf16),
            pltpu.VMEM((cols, LAYERS, width, full), bf16),
            pltpu.VMEM((own, tokens, full), f32),
            pltpu.VMEM((cols, tokens + 16, chans), bf16),
            pltpu.VMEM((samples, tokens, width), bf16),
            pltpu.VMEM((cols, own, tokens, width), bf16),
            pltpu.VMEM((rows, 8, tokens), f32),
            pltpu.VMEM((own, depth, width), bf16),
            pltpu.VMEM((own, depth, width), bf16),
            pltpu.VMEM((own, depth, width), bf16),
            pltpu.VMEM((own, depth, width), f32),
            pltpu.VMEM((LAYERS, rows, own, tokens, width), bf16),
            pltpu.VMEM((LAYERS, cols, own, tokens, width), bf16),
            pltpu.VMEM((cols, own, tokens, width), bf16),
            dma((2, cols)),
            dma((2, rows)),
            dma((2, LAYERS, cols)),
            dma((2, LAYERS, 2, rows)),
            dma((2, LAYERS, 3)),
            dma((2, max(rows, cols))),
            dma((2, LAYERS, own, 3)),
            dma((2, LAYERS, cols)),
            dma((2, max(rows, cols))),
        ],
        compiler_params=pltpu.CompilerParams(
            collective_id=0, has_side_effects=True, vmem_limit_bytes=56 * 1024 * 1024
        ),
        name="fused_blocks",
    )(
        biases,
        single,
        atom_feats,
        atom_token.reshape(1, slots),
        atom_count.reshape(1, 1),
        atom_weight,
        mask,
        qkvg_weight,
        out_weight,
    )


def solution(mesh):
    rows, cols = mesh.shape["row"], mesh.shape["col"]
    placed = (
        P(None, ("parts", "row"), "col"),
        P(("parts", "row"), "col", None),
        P(("parts", "row")),
        P(("parts", "row", "col"), None),
        P(("parts", "row", "col")),
        P(("parts", "row", "col")),
        P(None, "col"),
        P(),
        P(None, None, "col", None),
        P(None, "col", None),
    )

    def body(single, *rest):
        pairs = rest[0].shape
        square = rows == cols == 4 and single.shape[0] % rows == 0 and pairs[0] == pairs[1]
        if square and single.shape[2] % HEAD_DIM == 0:
            return per_device_fused(rows, cols, single, *rest)
        return per_device(single, *rest)

    return jax.shard_map(
        body,
        mesh=mesh,
        in_specs=placed,
        out_specs=P(None, ("parts", "row"), "col"),
        check_vma=False,
    )
```

```python
import math

import jax
import jax.numpy as jnp
from jax import lax
from jax.experimental import pallas as pl
from jax.experimental.pallas import tpu as pltpu
from jax.sharding import PartitionSpec as P

HEAD_DIM = 48
LAYERS = 2


EPS = 1e-05
MASKED = -1000000000.0
START_LOW = -1e30


def layer_norm(values):
    average = jnp.mean(values, axis=-1, keepdims=True)
    centered = values - average
    variance = jnp.mean(centered * centered, axis=-1, keepdims=True)
    return centered * lax.rsqrt(variance + EPS)


def per_device(
    single,
    pair_act,
    token_mask,
    atom_feats,
    atom_token,
    atom_count,
    atom_weight,
    bias_weight,
    qkvg_weight,
    out_weight,
):
    tok_rows = single.shape[1]
    sample_count = single.shape[0]
    slot_ids = jnp.arange(atom_feats.shape[0], dtype=jnp.int32)
    live_slots = slot_ids < atom_count[0]
    token_ids = jnp.arange(tok_rows, dtype=jnp.int32)
    owner_match = (token_ids[:, None] == atom_token[None, :]) & live_slots[None, :]
    owners = owner_match.astype(jnp.float32)
    counts = jnp.sum(owners, axis=1)
    atom_sums = jnp.dot(
        owner_match.astype(jnp.bfloat16), atom_feats, preferred_element_type=jnp.float32
    )
    sum_total, count_total = (
        lax.psum(atom_sums.astype(jnp.bfloat16), "col").astype(jnp.float32),
        lax.psum(counts[:, None].astype(jnp.bfloat16), "col").astype(jnp.float32),
    )
    pooled = (
        jnp.dot(sum_total, atom_weight.astype(jnp.float32), precision=lax.Precision.HIGHEST)
        / count_total
    )
    stream = (single.astype(jnp.float32) + pooled[None]).astype(jnp.bfloat16)
    pair_normed = layer_norm(pair_act.astype(jnp.float32)).astype(jnp.bfloat16)
    biases = jnp.einsum(
        "ijc,clh->lhij", pair_normed, bias_weight, preferred_element_type=jnp.float32
    ).astype(jnp.bfloat16)
    live_keys = (token_mask > 0).astype(jnp.bfloat16)[None, :]
    score_scale = 1.0 / math.sqrt(HEAD_DIM)
    for layer_idx in range(LAYERS):
        spread = lax.all_to_all(biases[layer_idx], "col", split_axis=0, concat_axis=2, tiled=True)
        gathered = lax.all_gather(stream, "col", axis=2, tiled=True)
        normed = layer_norm(gathered.astype(jnp.float32)).astype(jnp.bfloat16)
        projected = jnp.einsum(
            "std,fed->fste", normed, qkvg_weight[layer_idx], preferred_element_type=jnp.float32
        )
        head_width = projected.shape[3]
        heads_here = head_width // HEAD_DIM
        queries = (
            projected[0].astype(jnp.bfloat16).reshape(sample_count, tok_rows, heads_here, HEAD_DIM)
        )
        key_rows = projected[1].astype(jnp.bfloat16)
        value_rows = projected[2].astype(jnp.bfloat16)
        gating = jax.nn.sigmoid(projected[3])

        def attend(running, incoming, offset, queries=queries, spread=spread):
            top_old, summed_old, acc_old = running
            keys_in, values_in, live_in = incoming
            key_count = keys_in.shape[1]
            keys_heads = keys_in.reshape(sample_count, key_count, heads_here, HEAD_DIM)
            values_heads = values_in.reshape(sample_count, key_count, heads_here, HEAD_DIM)
            scores = (
                jnp.einsum(
                    "sqhd,skhd->shqk", queries, keys_heads, preferred_element_type=jnp.float32
                )
                * score_scale
            )
            scores = scores + spread.astype(jnp.float32)[None]
            scores = jnp.where(live_in[0][None, None, None, :] > 0, scores, MASKED)
            top_new = jnp.maximum(top_old, jnp.max(scores, axis=-1))
            exponent = jnp.exp(scores - top_new[..., None])
            summed_new = jnp.sum(exponent, axis=-1)
            weights = exponent.astype(jnp.bfloat16)
            acc_new = jnp.einsum(
                "shqk,skhd->shqd", weights, values_heads, preferred_element_type=jnp.float32
            )
            return (top_new, summed_new, acc_new)

        start_state = (
            jnp.full((sample_count, heads_here, tok_rows), START_LOW, jnp.float32),
            jnp.zeros((sample_count, heads_here, tok_rows), jnp.float32),
            jnp.zeros((sample_count, heads_here, tok_rows, HEAD_DIM), jnp.float32),
        )
        top_end, summed_end, acc_end = attend(
            start_state,
            (
                lax.all_gather(key_rows, "row", axis=1, tiled=True),
                lax.all_gather(value_rows, "row", axis=1, tiled=True),
                lax.all_gather(live_keys, "row", axis=1, tiled=True),
            ),
            jnp.int32(0),
        )
        attended = acc_end / summed_end[..., None]
        attended = attended.transpose(0, 2, 1, 3).reshape(sample_count, tok_rows, head_width)
        gated = (gating * attended).astype(jnp.bfloat16)
        out_rows = out_weight[layer_idx]

        def project(summed, incoming, offset, out_rows=out_rows):
            return jnp.einsum("std,ed->ste", incoming, out_rows, preferred_element_type=jnp.float32)

        zero_update = jnp.zeros((sample_count, tok_rows, out_rows.shape[0]), jnp.float32)
        update = project(
            zero_update, lax.all_gather(gated, "col", axis=2, tiled=True), jnp.int32(0)
        )
        stream = (stream.astype(jnp.float32) + update).astype(jnp.bfloat16)
    return stream


MESH = pl.DeviceIdType.MESH
NT = (((1,), (1,)), ((), ()))


def remote(src, dst, send_sem, recv_sem, row, col):
    return pltpu.make_async_remote_copy(
        src_ref=src,
        dst_ref=dst,
        send_sem=send_sem,
        recv_sem=recv_sem,
        device_id={"row": row, "col": col},
        device_id_type=MESH,
    )


def fused(
    rows,
    cols,
    bias,
    single,
    feats,
    slot_token,
    slot_count,
    atom_weight,
    mask,
    qkvg,
    out_w,
    out,
    spread,
    normed,
    out_full,
    stream,
    parts_buf,
    stream_send,
    stream_recv,
    mask_buf,
    queries,
    keys,
    values,
    gates,
    gated_send,
    gated_recv,
    final_send,
    part_sems,
    mask_sems,
    a2a_sems,
    ring_sems,
    out_w_sems,
    in_sems,
    ag_sems,
    gated_sems,
    end_sems,
):
    r = lax.axis_index("row")
    c = lax.axis_index("col")
    own = single.shape[0] // rows
    tokens = single.shape[2]
    width = single.shape[1]
    heads = width // HEAD_DIM
    sibling = c + 1 - 2 * lax.rem(c, 2)
    across = lax.rem(c + 2, cols)
    far = lax.rem(sibling + 2, cols)
    on_diag = r == c

    barrier = pltpu.get_barrier_semaphore()
    for dr in range(rows):
        for dc in range(cols):
            if dr or dc:
                pl.semaphore_signal(
                    barrier,
                    inc=1,
                    device_id={"row": lax.rem(r + dr, rows), "col": lax.rem(c + dc, cols)},
                    device_id_type=MESH,
                )
    pl.semaphore_wait(barrier, rows * cols - 1)

    sent = []

    def col_of(d):
        return lax.rem(c + d, cols)

    def bias_exchange(l):
        for d in range(1, cols):
            to = col_of(d)
            desc = remote(
                bias.at[l, to],
                spread.at[l, r, c],
                a2a_sems.at[0, l, d],
                a2a_sems.at[1, l, d],
                r,
                to,
            )
            desc.start()
            sent.append(desc)
        spread[l, r, c] = bias[l, c]

    def bias_exchange_wait(l):
        for d in range(1, cols):
            frm = col_of(cols - d)
            remote(
                bias.at[l, frm],
                spread.at[l, r, frm],
                a2a_sems.at[0, l, d],
                a2a_sems.at[1, l, d],
                r,
                frm,
            ).wait_recv()

    def ring_desc(l, right, step, block):
        side = 0 if right else 1
        to = r + 1 if right else r - 1
        return remote(
            spread.at[l, block],
            spread.at[l, block],
            ring_sems.at[0, l, side, step],
            ring_sems.at[1, l, side, step],
            to,
            c,
        )

    def ring_send(l, step):
        @pl.when((r + 1 < rows) & (r - step >= 0))
        def _():
            ring_desc(l, True, step, r - step).start()

        @pl.when((r - 1 >= 0) & (r + step < rows))
        def _():
            ring_desc(l, False, step, r + step).start()

    def ring_sent(l, step):
        @pl.when((r + 1 < rows) & (r - step >= 0))
        def _():
            ring_desc(l, True, step, r - step).wait_send()

        @pl.when((r - 1 >= 0) & (r + step < rows))
        def _():
            ring_desc(l, False, step, r + step).wait_send()

    def advance(l, step):
        @pl.when(r - 1 - step >= 0)
        def _():
            block = r - 1 - step
            remote(
                spread.at[l, block],
                spread.at[l, block],
                ring_sems.at[0, l, 0, step],
                ring_sems.at[1, l, 0, step],
                r - 1,
                c,
            ).wait_recv()

        @pl.when((r - 1 - step >= 0) & (r + 1 < rows) & (step + 1 < rows - 1))
        def _():
            ring_desc(l, True, step + 1, r - step - 1).start()

        @pl.when(r + 1 + step < rows)
        def _():
            block = r + 1 + step
            remote(
                spread.at[l, block],
                spread.at[l, block],
                ring_sems.at[0, l, 1, step],
                ring_sems.at[1, l, 1, step],
                r + 1,
                c,
            ).wait_recv()

        @pl.when((r + 1 + step < rows) & (r - 1 >= 0) & (step + 1 < rows - 1))
        def _():
            ring_desc(l, False, step + 1, r + step + 1).start()

    for d in range(1, rows):
        to = lax.rem(r + d, rows)
        desc = remote(mask, mask_buf.at[r], mask_sems.at[0, d], mask_sems.at[1, d], to, c)
        desc.start()
        sent.append(desc)
    mask_buf[r] = mask[...]

    slots = feats.shape[0]
    token_ids = lax.broadcasted_iota(jnp.int32, (tokens, slots), 0)
    slot_ids = lax.broadcasted_iota(jnp.int32, (tokens, slots), 1)
    match = (token_ids == slot_token[...]) & (slot_ids < slot_count[...])
    owners = jnp.where(match, 1.0, 0.0).astype(jnp.bfloat16)
    parts_buf[c, 0:tokens] = jnp.dot(
        owners, feats[...], preferred_element_type=jnp.float32
    ).astype(jnp.bfloat16)
    parts_buf[c, tokens : tokens + 16] = lax.dot_general(
        jnp.ones((16, slots), jnp.bfloat16), owners, NT, preferred_element_type=jnp.float32
    ).astype(jnp.bfloat16)
    for d in range(1, cols):
        desc = remote(
            parts_buf.at[c], parts_buf.at[c], part_sems.at[0, d], part_sems.at[1, d], r, col_of(d)
        )
        desc.start()
        sent.append(desc)
    bias_exchange(0)
    for d in range(1, cols):
        frm = col_of(cols - d)
        remote(
            parts_buf.at[frm], parts_buf.at[frm], part_sems.at[0, d], part_sems.at[1, d], r, frm
        ).wait_recv()
    total = jnp.zeros((width, tokens), jnp.float32)
    count_row = jnp.zeros((1, tokens), jnp.float32)
    for k in range(cols):
        total = total + lax.dot_general(
            atom_weight[...], parts_buf[k, 0:tokens], NT, preferred_element_type=jnp.float32
        )
        count_row = count_row + parts_buf[k, tokens : tokens + 16].astype(jnp.float32)[0:1]
    pooled = total / count_row
    for s in range(single.shape[0]):
        stream_send[s] = (single[s].astype(jnp.float32) + pooled).astype(jnp.bfloat16)
    for d in range(rows):
        to = lax.rem(r + d, rows)
        piece = stream_send.at[pl.ds(to * own, own)]
        if d == 0:

            @pl.when(on_diag)
            def _():
                stream_recv[c] = stream_send[pl.ds(r * own, own)]

            @pl.when(jnp.logical_not(on_diag))
            def _(piece=piece, to=to):
                remote(piece, stream_recv.at[c], in_sems.at[0, 0], in_sems.at[1, c], to, r).start()

        else:
            desc = remote(piece, stream_recv.at[c], in_sems.at[0, d], in_sems.at[1, c], to, r)
            desc.start()
            sent.append(desc)

    bias_exchange_wait(0)
    ring_send(0, 0)

    def out_w_send(l):
        for kind, to in ((0, sibling), (1, across)):
            desc = remote(
                out_w.at[l],
                out_full.at[c, l],
                out_w_sems.at[0, l, kind],
                out_w_sems.at[1, l, kind],
                r,
                to,
            )
            desc.start()
            sent.append(desc)
        out_full[c, l] = out_w[l]

    def out_w_arrived(l, kind, block):
        remote(
            out_w.at[l],
            out_full.at[block, l],
            out_w_sems.at[0, l, kind],
            out_w_sems.at[1, l, kind],
            r,
            sibling,
        ).wait_recv()

    for f in range(cols):

        @pl.when(jnp.logical_not(on_diag & (c == f)))
        def _(f=f):
            remote(
                stream_recv.at[f],
                stream_recv.at[f],
                in_sems.at[0, 0],
                in_sems.at[1, f],
                c,
                f,
            ).wait_recv()

    def send_normed(l, s, here):
        average = jnp.mean(here, axis=0, keepdims=True)
        centered = here - average
        variance = jnp.mean(centered * centered, axis=0, keepdims=True)
        normed[l, s, c] = (centered * lax.rsqrt(variance + EPS)).astype(jnp.bfloat16)
        for kind, to in ((0, sibling), (1, across)):
            desc = remote(
                normed.at[l, s, c],
                normed.at[l, s, c],
                ag_sems.at[0, l, s, kind],
                ag_sems.at[1, l, s, kind],
                r,
                to,
            )
            desc.start()
            sent.append(desc)

    def forward_normed(l, s):
        remote(
            normed.at[l, s, across],
            normed.at[l, s, across],
            ag_sems.at[0, l, s, 1],
            ag_sems.at[1, l, s, 1],
            r,
            across,
        ).wait_recv()
        desc = remote(
            normed.at[l, s, across],
            normed.at[l, s, across],
            ag_sems.at[0, l, s, 2],
            ag_sems.at[1, l, s, 2],
            r,
            sibling,
        )
        desc.start()
        sent.append(desc)

    def project(l, s):
        for kind, block in ((0, sibling), (2, far)):
            remote(
                normed.at[l, s, block],
                normed.at[l, s, block],
                ag_sems.at[0, l, s, kind],
                ag_sems.at[1, l, s, kind],
                r,
                sibling,
            ).wait_recv()
        here = jnp.concatenate([normed[l, s, k] for k in range(cols)], axis=1)

        def rows_of(f):
            return jnp.dot(qkvg[l, f], here, preferred_element_type=jnp.float32)

        keys[s] = rows_of(1).astype(jnp.bfloat16)
        values[s] = rows_of(2).astype(jnp.bfloat16)
        query = rows_of(0)
        gating = jax.nn.sigmoid(rows_of(3))
        for k in range(cols):
            at = slice(k * tokens, (k + 1) * tokens)
            queries[s, k] = query[:, at].T.astype(jnp.bfloat16)
            gates[s, k] = gating[:, at]

    score_scale = 1.0 / math.sqrt(HEAD_DIM)

    def attend(l, block):
        live = jnp.concatenate([mask_buf[k][0:1] for k in range(rows)], axis=1) > 0
        square = lax.broadcasted_iota(jnp.int32, (tokens, tokens), 0) == lax.broadcasted_iota(
            jnp.int32, (tokens, tokens), 1
        )

        def one_sample(s, carry):
            for h in range(heads):
                at = slice(h * HEAD_DIM, (h + 1) * HEAD_DIM)
                scores = (
                    jnp.dot(
                        queries[s, block, :, at], keys[s, at], preferred_element_type=jnp.float32
                    )
                    * score_scale
                )
                head_bias = jnp.concatenate([spread[l, block, k, h] for k in range(cols)], axis=1)
                scores = scores + head_bias.astype(jnp.float32)
                scores = jnp.where(live, scores, MASKED)
                highest = jnp.max(scores, axis=-1, keepdims=True)
                exponent = jnp.exp(scores - highest)
                summed = jnp.sum(exponent, axis=-1, keepdims=True)
                mixed = lax.dot_general(
                    values[s, at],
                    exponent.astype(jnp.bfloat16),
                    NT,
                    preferred_element_type=jnp.float32,
                )
                summed_row = jnp.sum(jnp.where(square, summed, 0.0), axis=0, keepdims=True)
                attended = mixed * (1.0 / summed_row)
                gated_send[l, block, s, at] = (gates[s, block, at] * attended).astype(jnp.bfloat16)
            return carry

        lax.fori_loop(0, own, one_sample, 0)

        gap = lax.rem(block - c + cols, cols)

        @pl.when(block != c)
        def _():
            remote(
                gated_send.at[l, block],
                gated_recv.at[l, c],
                gated_sems.at[0, l, gap],
                gated_sems.at[1, l, gap],
                r,
                block,
            ).start()

        @pl.when(block == c)
        def _():
            gated_recv[l, c] = gated_send[l, block]

    def gated_wait(l):
        for d in range(1, cols):
            frm = col_of(cols - d)
            remote(
                gated_send.at[l, frm],
                gated_recv.at[l, frm],
                gated_sems.at[0, l, d],
                gated_sems.at[1, l, d],
                r,
                frm,
            ).wait_recv()

    for d in range(1, rows):
        frm = lax.rem(r + rows - d, rows)
        remote(
            mask, mask_buf.at[frm], mask_sems.at[0, d], mask_sems.at[1, d], frm, c
        ).wait_recv()

    for s in range(own):
        here = jnp.concatenate([stream_recv[f, s].astype(jnp.float32) for f in range(cols)], axis=0)
        stream[s] = here
        send_normed(0, s, here)

    for l in range(LAYERS):
        for s in range(own):
            forward_normed(l, s)
            if s == 0:
                advance(l, 0)
        if l + 1 < LAYERS:
            bias_exchange(l + 1)
        out_w_send(l)
        for s in range(own):
            project(l, s)

        def ring_round(t, carry, l=l):
            def side(k, inner):
                block = r - t + 2 * t * k

                @pl.when((block >= 0) & (block < rows) & (k <= t))
                def _():
                    attend(l, block)

                return inner

            lax.fori_loop(0, 2, side, 0)

            @pl.when((t >= 1) & (t < rows - 1))
            def _():
                advance(l, t)

            @pl.when(t == rows - 2)
            def _():
                if l + 1 < LAYERS:
                    bias_exchange_wait(l + 1)
                    ring_send(l + 1, 0)

            @pl.when(t == 1)
            def _():
                out_w_arrived(l, 1, across)
                remote(
                    out_full.at[across, l],
                    out_full.at[across, l],
                    out_w_sems.at[0, l, 2],
                    out_w_sems.at[1, l, 2],
                    r,
                    sibling,
                ).start()

            return carry

        lax.fori_loop(0, rows, ring_round, 0)
        out_w_arrived(l, 0, sibling)
        out_w_arrived(l, 2, far)
        gated_wait(l)
        joined = jnp.concatenate(
            [
                jnp.concatenate([gated_recv[l, k, s] for k in range(cols)], axis=0)
                for s in range(own)
            ],
            axis=1,
        )
        weight = jnp.concatenate([out_full[k, l] for k in range(cols)], axis=0)
        update = jnp.dot(weight, joined, preferred_element_type=jnp.float32)
        for s in range(own):
            here = stream[s] + update[:, s * tokens : (s + 1) * tokens]
            rounded = here.astype(jnp.bfloat16)
            here = rounded.astype(jnp.float32)
            if l + 1 < LAYERS:
                stream[s] = here
                send_normed(l + 1, s, here)
            else:
                for f in range(cols):
                    final_send[f, s] = here[f * width : (f + 1) * width].astype(jnp.bfloat16)

    place = pl.ds(r * own, own)

    def end_desc(f):
        return remote(final_send.at[f], out.at[place], end_sems.at[0, f], end_sems.at[1, r], c, f)

    for f in range(cols):
        stays = on_diag & (c == f)

        @pl.when(stays)
        def _(f=f):
            out[place] = final_send[f]

        @pl.when(jnp.logical_not(stays))
        def _(f=f):
            end_desc(f).start()

    for k in range(rows):

        @pl.when(jnp.logical_not(on_diag & (r == k)))
        def _(k=k):
            remote(
                final_send.at[0],
                out.at[pl.ds(k * own, own)],
                end_sems.at[0, 0],
                end_sems.at[1, k],
                k,
                r,
            ).wait_recv()

    for f in range(cols):

        @pl.when(jnp.logical_not(on_diag & (c == f)))
        def _(f=f):
            end_desc(f).wait_send()

    for desc in sent:
        desc.wait_send()

    @pl.when(jnp.logical_not(on_diag))
    def _():
        remote(
            stream_send.at[pl.ds(r * own, own)],
            stream_recv.at[c],
            in_sems.at[0, 0],
            in_sems.at[1, c],
            r,
            r,
        ).wait_send()

    for l in range(LAYERS):
        remote(
            out_full.at[across, l],
            out_full.at[across, l],
            out_w_sems.at[0, l, 2],
            out_w_sems.at[1, l, 2],
            r,
            sibling,
        ).wait_send()
        for step in range(rows - 1):
            ring_sent(l, step)
        for d in range(1, cols):
            to = col_of(d)
            remote(
                gated_send.at[l, to],
                gated_recv.at[l, c],
                gated_sems.at[0, l, d],
                gated_sems.at[1, l, d],
                r,
                to,
            ).wait_send()


def per_device_fused(
    rows,
    cols,
    single,
    pair_act,
    token_mask,
    atom_feats,
    atom_token,
    atom_count,
    atom_weight,
    bias_weight,
    qkvg_weight,
    out_weight,
):
    samples, tokens, width = single.shape
    single = single.transpose(0, 2, 1)
    own = samples // rows
    depth = rows * tokens
    heads = width // HEAD_DIM
    full = width * cols
    chans = atom_feats.shape[1]
    slots = atom_feats.shape[0]
    pair_normed = layer_norm(pair_act.astype(jnp.float32)).astype(jnp.bfloat16)
    biases = (
        jnp.einsum("ijc,clh->lhij", pair_normed, bias_weight, preferred_element_type=jnp.float32)
        .astype(jnp.bfloat16)
        .reshape(LAYERS, cols, heads, tokens, tokens)
    )
    mask = jnp.broadcast_to((token_mask > 0).astype(jnp.float32)[None, :], (8, tokens))
    bf16, f32 = jnp.bfloat16, jnp.float32
    dma = pltpu.SemaphoreType.DMA
    updated = pl.pallas_call(
        lambda *refs: fused(rows, cols, *refs),
        out_shape=jax.ShapeDtypeStruct(single.shape, bf16),
        in_specs=[pl.BlockSpec(memory_space=pltpu.VMEM)] * 9,
        out_specs=pl.BlockSpec(memory_space=pltpu.VMEM),
        scratch_shapes=[
            pltpu.VMEM((LAYERS, rows, cols, heads, tokens, tokens), bf16),
            pltpu.VMEM((LAYERS, own, cols, full, tokens), bf16),
            pltpu.VMEM((cols, LAYERS, width, full), bf16),
            pltpu.VMEM((own, full, tokens), f32),
            pltpu.VMEM((cols, tokens + 16, chans), bf16),
            pltpu.VMEM((samples, width, tokens), bf16),
            pltpu.VMEM((cols, own, width, tokens), bf16),
            pltpu.VMEM((rows, 8, tokens), f32),
            pltpu.VMEM((own, rows, tokens, width), bf16),
            pltpu.VMEM((own, width, depth), bf16),
            pltpu.VMEM((own, width, depth), bf16),
            pltpu.VMEM((own, rows, width, tokens), f32),
            pltpu.VMEM((LAYERS, rows, own, width, tokens), bf16),
            pltpu.VMEM((LAYERS, cols, own, width, tokens), bf16),
            pltpu.VMEM((cols, own, width, tokens), bf16),
            dma((2, cols)),
            dma((2, rows)),
            dma((2, LAYERS, cols)),
            dma((2, LAYERS, 2, rows)),
            dma((2, LAYERS, 3)),
            dma((2, max(rows, cols))),
            dma((2, LAYERS, own, 3)),
            dma((2, LAYERS, cols)),
            dma((2, max(rows, cols))),
        ],
        compiler_params=pltpu.CompilerParams(
            collective_id=0, has_side_effects=True, vmem_limit_bytes=56 * 1024 * 1024
        ),
        name="fused_blocks",
    )(
        biases,
        single,
        atom_feats,
        atom_token.reshape(1, slots),
        atom_count.reshape(1, 1),
        atom_weight.T,
        mask,
        qkvg_weight,
        out_weight,
    )
    return updated.transpose(0, 2, 1)


def solution(mesh):
    rows, cols = mesh.shape["row"], mesh.shape["col"]
    placed = (
        P(None, ("parts", "row"), "col"),
        P(("parts", "row"), "col", None),
        P(("parts", "row")),
        P(("parts", "row", "col"), None),
        P(("parts", "row", "col")),
        P(("parts", "row", "col")),
        P(None, "col"),
        P(),
        P(None, None, "col", None),
        P(None, "col", None),
    )

    def body(single, *rest):
        pairs = rest[0].shape
        square = rows == cols == 4 and single.shape[0] % rows == 0 and pairs[0] == pairs[1]
        if square and single.shape[2] % HEAD_DIM == 0:
            return per_device_fused(rows, cols, single, *rest)
        return per_device(single, *rest)

    return jax.shard_map(
        body,
        mesh=mesh,
        in_specs=placed,
        out_specs=P(None, ("parts", "row"), "col"),
        check_vma=False,
    )
```

```python
import math

import jax
import jax.numpy as jnp
from jax import lax
from jax.experimental import pallas as pl
from jax.experimental.pallas import tpu as pltpu
from jax.sharding import PartitionSpec as P

HEAD_DIM = 48
LAYERS = 2


EPS = 1e-05
MASKED = -1000000000.0
START_LOW = -1e30


def layer_norm(values):
    average = jnp.mean(values, axis=-1, keepdims=True)
    centered = values - average
    variance = jnp.mean(centered * centered, axis=-1, keepdims=True)
    return centered * lax.rsqrt(variance + EPS)


def per_device(
    single,
    pair_act,
    token_mask,
    atom_feats,
    atom_token,
    atom_count,
    atom_weight,
    bias_weight,
    qkvg_weight,
    out_weight,
):
    tok_rows = single.shape[1]
    sample_count = single.shape[0]
    slot_ids = jnp.arange(atom_feats.shape[0], dtype=jnp.int32)
    live_slots = slot_ids < atom_count[0]
    token_ids = jnp.arange(tok_rows, dtype=jnp.int32)
    owner_match = (token_ids[:, None] == atom_token[None, :]) & live_slots[None, :]
    owners = owner_match.astype(jnp.float32)
    counts = jnp.sum(owners, axis=1)
    atom_sums = jnp.dot(
        owner_match.astype(jnp.bfloat16), atom_feats, preferred_element_type=jnp.float32
    )
    sum_total, count_total = (
        lax.psum(atom_sums.astype(jnp.bfloat16), "col").astype(jnp.float32),
        lax.psum(counts[:, None].astype(jnp.bfloat16), "col").astype(jnp.float32),
    )
    pooled = (
        jnp.dot(sum_total, atom_weight.astype(jnp.float32), precision=lax.Precision.HIGHEST)
        / count_total
    )
    stream = (single.astype(jnp.float32) + pooled[None]).astype(jnp.bfloat16)
    pair_normed = layer_norm(pair_act.astype(jnp.float32)).astype(jnp.bfloat16)
    biases = jnp.einsum(
        "ijc,clh->lhij", pair_normed, bias_weight, preferred_element_type=jnp.float32
    ).astype(jnp.bfloat16)
    live_keys = (token_mask > 0).astype(jnp.bfloat16)[None, :]
    score_scale = 1.0 / math.sqrt(HEAD_DIM)
    for layer_idx in range(LAYERS):
        spread = lax.all_to_all(biases[layer_idx], "col", split_axis=0, concat_axis=2, tiled=True)
        gathered = lax.all_gather(stream, "col", axis=2, tiled=True)
        normed = layer_norm(gathered.astype(jnp.float32)).astype(jnp.bfloat16)
        projected = jnp.einsum(
            "std,fed->fste", normed, qkvg_weight[layer_idx], preferred_element_type=jnp.float32
        )
        head_width = projected.shape[3]
        heads_here = head_width // HEAD_DIM
        queries = (
            projected[0].astype(jnp.bfloat16).reshape(sample_count, tok_rows, heads_here, HEAD_DIM)
        )
        key_rows = projected[1].astype(jnp.bfloat16)
        value_rows = projected[2].astype(jnp.bfloat16)
        gating = jax.nn.sigmoid(projected[3])

        def attend(running, incoming, offset, queries=queries, spread=spread):
            top_old, summed_old, acc_old = running
            keys_in, values_in, live_in = incoming
            key_count = keys_in.shape[1]
            keys_heads = keys_in.reshape(sample_count, key_count, heads_here, HEAD_DIM)
            values_heads = values_in.reshape(sample_count, key_count, heads_here, HEAD_DIM)
            scores = (
                jnp.einsum(
                    "sqhd,skhd->shqk", queries, keys_heads, preferred_element_type=jnp.float32
                )
                * score_scale
            )
            scores = scores + spread.astype(jnp.float32)[None]
            scores = jnp.where(live_in[0][None, None, None, :] > 0, scores, MASKED)
            top_new = jnp.maximum(top_old, jnp.max(scores, axis=-1))
            exponent = jnp.exp(scores - top_new[..., None])
            summed_new = jnp.sum(exponent, axis=-1)
            weights = exponent.astype(jnp.bfloat16)
            acc_new = jnp.einsum(
                "shqk,skhd->shqd", weights, values_heads, preferred_element_type=jnp.float32
            )
            return (top_new, summed_new, acc_new)

        start_state = (
            jnp.full((sample_count, heads_here, tok_rows), START_LOW, jnp.float32),
            jnp.zeros((sample_count, heads_here, tok_rows), jnp.float32),
            jnp.zeros((sample_count, heads_here, tok_rows, HEAD_DIM), jnp.float32),
        )
        top_end, summed_end, acc_end = attend(
            start_state,
            (
                lax.all_gather(key_rows, "row", axis=1, tiled=True),
                lax.all_gather(value_rows, "row", axis=1, tiled=True),
                lax.all_gather(live_keys, "row", axis=1, tiled=True),
            ),
            jnp.int32(0),
        )
        attended = acc_end / summed_end[..., None]
        attended = attended.transpose(0, 2, 1, 3).reshape(sample_count, tok_rows, head_width)
        gated = (gating * attended).astype(jnp.bfloat16)
        out_rows = out_weight[layer_idx]

        def project(summed, incoming, offset, out_rows=out_rows):
            return jnp.einsum("std,ed->ste", incoming, out_rows, preferred_element_type=jnp.float32)

        zero_update = jnp.zeros((sample_count, tok_rows, out_rows.shape[0]), jnp.float32)
        update = project(
            zero_update, lax.all_gather(gated, "col", axis=2, tiled=True), jnp.int32(0)
        )
        stream = (stream.astype(jnp.float32) + update).astype(jnp.bfloat16)
    return stream


MESH = pl.DeviceIdType.MESH
NT = (((1,), (1,)), ((), ()))


def remote(src, dst, send_sem, recv_sem, row, col):
    return pltpu.make_async_remote_copy(
        src_ref=src,
        dst_ref=dst,
        send_sem=send_sem,
        recv_sem=recv_sem,
        device_id={"row": row, "col": col},
        device_id_type=MESH,
    )


def fused(
    rows,
    cols,
    bias,
    single,
    feats,
    slot_token,
    slot_count,
    atom_weight,
    mask,
    qkvg,
    out_w,
    out,
    spread,
    normed,
    out_full,
    stream,
    parts_buf,
    stream_send,
    stream_recv,
    mask_buf,
    queries,
    keys,
    values,
    gates,
    gated_send,
    gated_recv,
    final_send,
    part_sems,
    mask_sems,
    a2a_sems,
    ring_sems,
    out_w_sems,
    in_sems,
    ag_sems,
    gated_sems,
    end_sems,
):
    r = lax.axis_index("row")
    c = lax.axis_index("col")
    own = single.shape[0] // rows
    tokens = single.shape[2]
    width = single.shape[1]
    heads = width // HEAD_DIM
    sibling = c + 1 - 2 * lax.rem(c, 2)
    across = lax.rem(c + 2, cols)
    far = lax.rem(sibling + 2, cols)
    on_diag = r == c

    barrier = pltpu.get_barrier_semaphore()
    for dr in range(rows):
        for dc in range(cols):
            if dr or dc:
                pl.semaphore_signal(
                    barrier,
                    inc=1,
                    device_id={"row": lax.rem(r + dr, rows), "col": lax.rem(c + dc, cols)},
                    device_id_type=MESH,
                )
    pl.semaphore_wait(barrier, rows * cols - 1)

    sent = []

    def col_of(d):
        return lax.rem(c + d, cols)

    def bias_exchange(l):
        for d in range(1, cols):
            to = col_of(d)
            desc = remote(
                bias.at[l, to],
                spread.at[l, r, c],
                a2a_sems.at[0, l, d],
                a2a_sems.at[1, l, d],
                r,
                to,
            )
            desc.start()
            sent.append(desc)
        spread[l, r, c] = bias[l, c]

    def bias_exchange_wait(l):
        for d in range(1, cols):
            frm = col_of(cols - d)
            remote(
                bias.at[l, frm],
                spread.at[l, r, frm],
                a2a_sems.at[0, l, d],
                a2a_sems.at[1, l, d],
                r,
                frm,
            ).wait_recv()

    def ring_desc(l, right, step, block):
        side = 0 if right else 1
        to = r + 1 if right else r - 1
        return remote(
            spread.at[l, block],
            spread.at[l, block],
            ring_sems.at[0, l, side, step],
            ring_sems.at[1, l, side, step],
            to,
            c,
        )

    def ring_send(l, step):
        @pl.when((r + 1 < rows) & (r - step >= 0))
        def _():
            ring_desc(l, True, step, r - step).start()

        @pl.when((r - 1 >= 0) & (r + step < rows))
        def _():
            ring_desc(l, False, step, r + step).start()

    def ring_sent(l, step):
        @pl.when((r + 1 < rows) & (r - step >= 0))
        def _():
            ring_desc(l, True, step, r - step).wait_send()

        @pl.when((r - 1 >= 0) & (r + step < rows))
        def _():
            ring_desc(l, False, step, r + step).wait_send()

    def advance(l, step):
        @pl.when(r - 1 - step >= 0)
        def _():
            block = r - 1 - step
            remote(
                spread.at[l, block],
                spread.at[l, block],
                ring_sems.at[0, l, 0, step],
                ring_sems.at[1, l, 0, step],
                r - 1,
                c,
            ).wait_recv()

        @pl.when((r - 1 - step >= 0) & (r + 1 < rows) & (step + 1 < rows - 1))
        def _():
            ring_desc(l, True, step + 1, r - step - 1).start()

        @pl.when(r + 1 + step < rows)
        def _():
            block = r + 1 + step
            remote(
                spread.at[l, block],
                spread.at[l, block],
                ring_sems.at[0, l, 1, step],
                ring_sems.at[1, l, 1, step],
                r + 1,
                c,
            ).wait_recv()

        @pl.when((r + 1 + step < rows) & (r - 1 >= 0) & (step + 1 < rows - 1))
        def _():
            ring_desc(l, False, step + 1, r + step + 1).start()

    for d in range(1, rows):
        to = lax.rem(r + d, rows)
        desc = remote(mask, mask_buf.at[r], mask_sems.at[0, d], mask_sems.at[1, d], to, c)
        desc.start()
        sent.append(desc)
    mask_buf[r] = mask[...]

    slots = feats.shape[0]
    token_ids = lax.broadcasted_iota(jnp.int32, (tokens, slots), 0)
    slot_ids = lax.broadcasted_iota(jnp.int32, (tokens, slots), 1)
    match = (token_ids == slot_token[...]) & (slot_ids < slot_count[...])
    owners = jnp.where(match, 1.0, 0.0).astype(jnp.bfloat16)
    parts_buf[c, 0:tokens] = jnp.dot(
        owners, feats[...], preferred_element_type=jnp.float32
    ).astype(jnp.bfloat16)
    parts_buf[c, tokens : tokens + 16] = lax.dot_general(
        jnp.ones((16, slots), jnp.bfloat16), owners, NT, preferred_element_type=jnp.float32
    ).astype(jnp.bfloat16)
    for d in range(1, cols):
        desc = remote(
            parts_buf.at[c], parts_buf.at[c], part_sems.at[0, d], part_sems.at[1, d], r, col_of(d)
        )
        desc.start()
        sent.append(desc)
    bias_exchange(0)
    for d in range(1, cols):
        frm = col_of(cols - d)
        remote(
            parts_buf.at[frm], parts_buf.at[frm], part_sems.at[0, d], part_sems.at[1, d], r, frm
        ).wait_recv()
    total = jnp.zeros((width, tokens), jnp.float32)
    count_row = jnp.zeros((1, tokens), jnp.float32)
    for k in range(cols):
        total = total + lax.dot_general(
            atom_weight[...], parts_buf[k, 0:tokens], NT, preferred_element_type=jnp.float32
        )
        count_row = count_row + parts_buf[k, tokens : tokens + 16].astype(jnp.float32)[0:1]
    pooled = total / count_row
    for s in range(single.shape[0]):
        stream_send[s] = (single[s].astype(jnp.float32) + pooled).astype(jnp.bfloat16)
    for d in range(rows):
        to = lax.rem(r + d, rows)
        piece = stream_send.at[pl.ds(to * own, own)]
        if d == 0:

            @pl.when(on_diag)
            def _():
                stream_recv[c] = stream_send[pl.ds(r * own, own)]

            @pl.when(jnp.logical_not(on_diag))
            def _(piece=piece, to=to):
                remote(piece, stream_recv.at[c], in_sems.at[0, 0], in_sems.at[1, c], to, r).start()

        else:
            desc = remote(piece, stream_recv.at[c], in_sems.at[0, d], in_sems.at[1, c], to, r)
            desc.start()
            sent.append(desc)

    bias_exchange_wait(0)
    ring_send(0, 0)

    def out_w_send(l):
        for kind, to in ((0, sibling), (1, across)):
            desc = remote(
                out_w.at[l],
                out_full.at[c, l],
                out_w_sems.at[0, l, kind],
                out_w_sems.at[1, l, kind],
                r,
                to,
            )
            desc.start()
            sent.append(desc)
        out_full[c, l] = out_w[l]

    def out_w_arrived(l, kind, block):
        remote(
            out_w.at[l],
            out_full.at[block, l],
            out_w_sems.at[0, l, kind],
            out_w_sems.at[1, l, kind],
            r,
            sibling,
        ).wait_recv()

    for f in range(cols):

        @pl.when(jnp.logical_not(on_diag & (c == f)))
        def _(f=f):
            remote(
                stream_recv.at[f],
                stream_recv.at[f],
                in_sems.at[0, 0],
                in_sems.at[1, f],
                c,
                f,
            ).wait_recv()

    def send_normed(l, s, here):
        average = jnp.mean(here, axis=0, keepdims=True)
        centered = here - average
        variance = jnp.mean(centered * centered, axis=0, keepdims=True)
        normed[l, s, c] = (centered * lax.rsqrt(variance + EPS)).astype(jnp.bfloat16)
        for kind, to in ((0, sibling), (1, across)):
            desc = remote(
                normed.at[l, s, c],
                normed.at[l, s, c],
                ag_sems.at[0, l, s, kind],
                ag_sems.at[1, l, s, kind],
                r,
                to,
            )
            desc.start()
            sent.append(desc)

    def forward_normed(l, s):
        remote(
            normed.at[l, s, across],
            normed.at[l, s, across],
            ag_sems.at[0, l, s, 1],
            ag_sems.at[1, l, s, 1],
            r,
            across,
        ).wait_recv()
        desc = remote(
            normed.at[l, s, across],
            normed.at[l, s, across],
            ag_sems.at[0, l, s, 2],
            ag_sems.at[1, l, s, 2],
            r,
            sibling,
        )
        desc.start()
        sent.append(desc)

    def project(l, s):
        for kind, block in ((0, sibling), (2, far)):
            remote(
                normed.at[l, s, block],
                normed.at[l, s, block],
                ag_sems.at[0, l, s, kind],
                ag_sems.at[1, l, s, kind],
                r,
                sibling,
            ).wait_recv()
        here = jnp.concatenate([normed[l, s, k] for k in range(cols)], axis=1)

        def rows_of(f):
            return jnp.dot(qkvg[l, f], here, preferred_element_type=jnp.float32)

        keys[s] = rows_of(1).astype(jnp.bfloat16)
        values[s] = rows_of(2).astype(jnp.bfloat16)
        query = rows_of(0)
        gating = jax.nn.sigmoid(rows_of(3))
        for k in range(cols):
            at = slice(k * tokens, (k + 1) * tokens)
            queries[s, k] = query[:, at].T.astype(jnp.bfloat16)
            gates[s, k] = gating[:, at]

    score_scale = 1.0 / math.sqrt(HEAD_DIM)

    def attend(l, block):
        live = jnp.concatenate([mask_buf[k][0:1] for k in range(rows)], axis=1) > 0
        square = lax.broadcasted_iota(jnp.int32, (tokens, tokens), 0) == lax.broadcasted_iota(
            jnp.int32, (tokens, tokens), 1
        )

        def one_sample(s, carry):
            for h in range(heads):
                at = slice(h * HEAD_DIM, (h + 1) * HEAD_DIM)
                scores = (
                    jnp.dot(
                        queries[s, block, :, at], keys[s, at], preferred_element_type=jnp.float32
                    )
                    * score_scale
                )
                head_bias = jnp.concatenate([spread[l, block, k, h] for k in range(cols)], axis=1)
                scores = scores + head_bias.astype(jnp.float32)
                scores = jnp.where(live, scores, MASKED)
                highest = jnp.max(scores, axis=-1, keepdims=True)
                exponent = jnp.exp(scores - highest)
                summed = jnp.sum(exponent, axis=-1, keepdims=True)
                mixed = lax.dot_general(
                    values[s, at],
                    exponent.astype(jnp.bfloat16),
                    NT,
                    preferred_element_type=jnp.float32,
                )
                summed_row = jnp.sum(jnp.where(square, summed, 0.0), axis=0, keepdims=True)
                attended = mixed * (1.0 / summed_row)
                gated_send[l, block, s, at] = (gates[s, block, at] * attended).astype(jnp.bfloat16)
            return carry

        lax.fori_loop(0, own, one_sample, 0)

        gap = lax.rem(block - c + cols, cols)

        @pl.when(block != c)
        def _():
            remote(
                gated_send.at[l, block],
                gated_recv.at[l, c],
                gated_sems.at[0, l, gap],
                gated_sems.at[1, l, gap],
                r,
                block,
            ).start()

        @pl.when(block == c)
        def _():
            gated_recv[l, c] = gated_send[l, block]

    def gated_wait(l):
        for d in range(1, cols):
            frm = col_of(cols - d)
            remote(
                gated_send.at[l, frm],
                gated_recv.at[l, frm],
                gated_sems.at[0, l, d],
                gated_sems.at[1, l, d],
                r,
                frm,
            ).wait_recv()

    for d in range(1, rows):
        frm = lax.rem(r + rows - d, rows)
        remote(
            mask, mask_buf.at[frm], mask_sems.at[0, d], mask_sems.at[1, d], frm, c
        ).wait_recv()

    for s in range(own):
        here = jnp.concatenate([stream_recv[f, s].astype(jnp.float32) for f in range(cols)], axis=0)
        stream[s] = here
        send_normed(0, s, here)

    for l in range(LAYERS):
        for s in range(own):
            forward_normed(l, s)
            if s == 0:
                advance(l, 0)
        if l + 1 < LAYERS:
            bias_exchange(l + 1)
        out_w_send(l)
        for s in range(own):
            project(l, s)

        def ring_round(t, carry, l=l):
            def side(k, inner):
                block = r - t + 2 * t * k

                @pl.when((block >= 0) & (block < rows) & (k <= t))
                def _():
                    attend(l, block)

                return inner

            lax.fori_loop(0, 2, side, 0)

            @pl.when((t >= 1) & (t < rows - 1))
            def _():
                advance(l, t)

            @pl.when(t == rows - 2)
            def _():
                if l + 1 < LAYERS:
                    bias_exchange_wait(l + 1)
                    ring_send(l + 1, 0)

            @pl.when(t == 1)
            def _():
                out_w_arrived(l, 1, across)
                remote(
                    out_full.at[across, l],
                    out_full.at[across, l],
                    out_w_sems.at[0, l, 2],
                    out_w_sems.at[1, l, 2],
                    r,
                    sibling,
                ).start()

            return carry

        lax.fori_loop(0, rows, ring_round, 0)
        out_w_arrived(l, 0, sibling)
        out_w_arrived(l, 2, far)
        gated_wait(l)
        joined = jnp.concatenate(
            [
                jnp.concatenate([gated_recv[l, k, s] for k in range(cols)], axis=0)
                for s in range(own)
            ],
            axis=1,
        )
        weight = jnp.concatenate([out_full[k, l] for k in range(cols)], axis=0)
        update = jnp.dot(weight, joined, preferred_element_type=jnp.float32)
        for s in range(own):
            here = stream[s] + update[:, s * tokens : (s + 1) * tokens]
            rounded = here.astype(jnp.bfloat16)
            here = rounded.astype(jnp.float32)
            if l + 1 < LAYERS:
                stream[s] = here
                send_normed(l + 1, s, here)
            else:
                for f in range(cols):
                    final_send[f, s] = here[f * width : (f + 1) * width].astype(jnp.bfloat16)

    place = pl.ds(r * own, own)

    def end_desc(f):
        return remote(final_send.at[f], out.at[place], end_sems.at[0, f], end_sems.at[1, r], c, f)

    for f in range(cols):
        stays = on_diag & (c == f)

        @pl.when(stays)
        def _(f=f):
            out[place] = final_send[f]

        @pl.when(jnp.logical_not(stays))
        def _(f=f):
            end_desc(f).start()

    for k in range(rows):

        @pl.when(jnp.logical_not(on_diag & (r == k)))
        def _(k=k):
            remote(
                final_send.at[0],
                out.at[pl.ds(k * own, own)],
                end_sems.at[0, 0],
                end_sems.at[1, k],
                k,
                r,
            ).wait_recv()

    for f in range(cols):

        @pl.when(jnp.logical_not(on_diag & (c == f)))
        def _(f=f):
            end_desc(f).wait_send()

    for desc in sent:
        desc.wait_send()

    @pl.when(jnp.logical_not(on_diag))
    def _():
        remote(
            stream_send.at[pl.ds(r * own, own)],
            stream_recv.at[c],
            in_sems.at[0, 0],
            in_sems.at[1, c],
            r,
            r,
        ).wait_send()

    for l in range(LAYERS):
        remote(
            out_full.at[across, l],
            out_full.at[across, l],
            out_w_sems.at[0, l, 2],
            out_w_sems.at[1, l, 2],
            r,
            sibling,
        ).wait_send()
        for step in range(rows - 1):
            ring_sent(l, step)
        for d in range(1, cols):
            to = col_of(d)
            remote(
                gated_send.at[l, to],
                gated_recv.at[l, c],
                gated_sems.at[0, l, d],
                gated_sems.at[1, l, d],
                r,
                to,
            ).wait_send()


def pair_bias(x_ref, w_ref, o_ref):
    lines, across, chans = x_ref.shape
    here = x_ref[...].reshape(lines * across, chans).astype(jnp.float32)
    rounded = layer_norm(here).astype(jnp.bfloat16)
    biases = lax.dot_general(w_ref[...], rounded, NT, preferred_element_type=jnp.float32)
    o_ref[...] = biases.reshape(w_ref.shape[0], lines, across).astype(jnp.bfloat16)


def per_device_fused(
    rows,
    cols,
    single,
    pair_act,
    token_mask,
    atom_feats,
    atom_token,
    atom_count,
    atom_weight,
    bias_weight,
    qkvg_weight,
    out_weight,
):
    samples, tokens, width = single.shape
    single = single.transpose(0, 2, 1)
    own = samples // rows
    depth = rows * tokens
    heads = width // HEAD_DIM
    full = width * cols
    chans = atom_feats.shape[1]
    slots = atom_feats.shape[0]
    lines, pairs = 16, pair_act.shape[2]
    all_heads = bias_weight.shape[1] * bias_weight.shape[2]
    biases = pl.pallas_call(
        pair_bias,
        grid=(tokens // lines,),
        in_specs=[
            pl.BlockSpec((lines, tokens, pairs), lambda i: (i, 0, 0)),
            pl.BlockSpec((all_heads, pairs), lambda i: (0, 0)),
        ],
        out_specs=pl.BlockSpec((all_heads, lines, tokens), lambda i: (0, i, 0)),
        out_shape=jax.ShapeDtypeStruct((all_heads, tokens, tokens), jnp.bfloat16),
        name="pair_bias",
    )(pair_act, bias_weight.reshape(pairs, all_heads).T)
    biases = biases.reshape(LAYERS, cols, heads, tokens, tokens)
    mask = jnp.broadcast_to((token_mask > 0).astype(jnp.float32)[None, :], (8, tokens))
    bf16, f32 = jnp.bfloat16, jnp.float32
    dma = pltpu.SemaphoreType.DMA
    updated = pl.pallas_call(
        lambda *refs: fused(rows, cols, *refs),
        out_shape=jax.ShapeDtypeStruct(single.shape, bf16),
        in_specs=[pl.BlockSpec(memory_space=pltpu.VMEM)] * 9,
        out_specs=pl.BlockSpec(memory_space=pltpu.VMEM),
        scratch_shapes=[
            pltpu.VMEM((LAYERS, rows, cols, heads, tokens, tokens), bf16),
            pltpu.VMEM((LAYERS, own, cols, full, tokens), bf16),
            pltpu.VMEM((cols, LAYERS, width, full), bf16),
            pltpu.VMEM((own, full, tokens), f32),
            pltpu.VMEM((cols, tokens + 16, chans), bf16),
            pltpu.VMEM((samples, width, tokens), bf16),
            pltpu.VMEM((cols, own, width, tokens), bf16),
            pltpu.VMEM((rows, 8, tokens), f32),
            pltpu.VMEM((own, rows, tokens, width), bf16),
            pltpu.VMEM((own, width, depth), bf16),
            pltpu.VMEM((own, width, depth), bf16),
            pltpu.VMEM((own, rows, width, tokens), f32),
            pltpu.VMEM((LAYERS, rows, own, width, tokens), bf16),
            pltpu.VMEM((LAYERS, cols, own, width, tokens), bf16),
            pltpu.VMEM((cols, own, width, tokens), bf16),
            dma((2, cols)),
            dma((2, rows)),
            dma((2, LAYERS, cols)),
            dma((2, LAYERS, 2, rows)),
            dma((2, LAYERS, 3)),
            dma((2, max(rows, cols))),
            dma((2, LAYERS, own, 3)),
            dma((2, LAYERS, cols)),
            dma((2, max(rows, cols))),
        ],
        compiler_params=pltpu.CompilerParams(
            collective_id=0, has_side_effects=True, vmem_limit_bytes=56 * 1024 * 1024
        ),
        name="fused_blocks",
    )(
        biases,
        single,
        atom_feats,
        atom_token.reshape(1, slots),
        atom_count.reshape(1, 1),
        atom_weight.T,
        mask,
        qkvg_weight,
        out_weight,
    )
    return updated.transpose(0, 2, 1)


def solution(mesh):
    rows, cols = mesh.shape["row"], mesh.shape["col"]
    placed = (
        P(None, ("parts", "row"), "col"),
        P(("parts", "row"), "col", None),
        P(("parts", "row")),
        P(("parts", "row", "col"), None),
        P(("parts", "row", "col")),
        P(("parts", "row", "col")),
        P(None, "col"),
        P(),
        P(None, None, "col", None),
        P(None, "col", None),
    )

    def body(single, *rest):
        pairs = rest[0].shape
        square = rows == cols == 4 and single.shape[0] % rows == 0 and pairs[0] == pairs[1]
        square = square and pairs[0] % 128 == 0
        if square and single.shape[2] % HEAD_DIM == 0:
            return per_device_fused(rows, cols, single, *rest)
        return per_device(single, *rest)

    return jax.shard_map(
        body,
        mesh=mesh,
        in_specs=placed,
        out_specs=P(None, ("parts", "row"), "col"),
        check_vma=False,
    )
```
